32 devices in a mesh: groups: 2 (over y), wide: 4 (over x, core), tp: 4 (over z).
Axes of the slice: x: 2, y: 2, z: 4, core: 2. Of those that a mesh axis runs over, the one named last changes fastest.
Arguments:
- patches: bfloat16 [2048, 1280], P(('groups', 'wide')), parts along dimension 0, may hold values from -190 to 190
- patch_counts: int32 [64], P('groups'), parts along dimension 0, may hold values from 24 to 32, as said below
- placement: int32 [64, 2], P('groups'), parts along dimension 0, may hold values from 0 to 511, as said below
- positions: int32 [3, 4096], P(None, ('groups', 'wide')), parts along dimension 1, may hold values from 0 to 2047
- text_embeds: bfloat16 [4096, 8192], P(('groups', 'wide'), 'tp'), parts along dimension 0, may hold values from -180 to 180
- vit_gain: float32 [1280], replicated, may hold values from 0.1 to 1.9
- vit_qkv: bfloat16 [1280, 3, 1280], P(None, None, 'tp'), may hold values from -4 to 4
- vit_proj: bfloat16 [1280, 1280], P('tp'), may hold values from -0.15625 to 0.15625
- merger_gain: float32 [1280], replicated, may hold values from 0.1 to 1.9
- merger_up: bfloat16 [5120, 2560], P(None, 'tp'), may hold values from -0.078125 to 0.078125
- merger_down: bfloat16 [2560, 8192], P('tp'), may hold values from -0.15625 to 0.15625
- llm_gain: float32 [8192], replicated, may hold values from 0.1 to 1.9
- llm_query: bfloat16 [8192, 4096], P('wide', 'tp'), may hold values from -0.0625 to 0.0625
- llm_key: bfloat16 [8192, 1024], P('wide', 'tp'), may hold values from -0.0625 to 0.0625
- llm_value: bfloat16 [8192, 1024], P('wide', 'tp'), may hold values from -0.0625 to 0.0625
Outputs:
- query: bfloat16 [4096, 4096], P(('groups', 'wide'), 'tp'), parts along dimension 0
- key_cache: bfloat16 [4096, 1024], P(('groups', 'wide'), 'tp'), parts along dimension 0
- value_cache: bfloat16 [4096, 1024], P(('groups', 'wide'), 'tp'), parts along dimension 0
The draws below stay inside these ranges and needn't reach their ends.
There are 2 independent parts, one for each index of `groups`. The reference program is written for one: setup_inputs(seed, part) draws one part's arguments, and reference() takes and returns one part's arrays. A program takes and returns all parts, laid end to end along the dimension named above; an argument that names none is the same for every part. Nothing has to cross between parts.
Inputs may be any that keep to these rules, and one draw needn't show every extreme that they name: `patch_counts`: each count is a multiple of 4; images 8 * s to 8 * s + 7 belong to encoder device s of the wide axis; patch rows 4 m to 4 m + 3 of an image form its merged row m. `placement`: column 0 is the owner on the wide axis, column 1 the first of the image's merged rows among that owner's 512 rows. Images' merged rows never intersect and stay within the owner's rows. Each owner receives 8 images. At most 16 merged rows go from one encoder device to one owner, and that number is reached in every draw.
All inputs are finite; a program needn't handle non-finite values.
Results may differ from the reference program's by a relative error of at most 0.015.
Values may be sent and summed in bfloat16 or wider, within the bound.
No kernel may reach another device: no remote copies, remote signals or barrier semaphores. Data moves between devices by JAX's collectives and lax.ppermute only.
A program may use at most 128 MiB of HBM per device.

```python
import jax
import jax.numpy as jnp
from jax import lax

VD = 1280
VH = 16
LD = 8192
KVH = 8
HD = 128
QH = 32
MH = 2560
IMG_DEV = 8
MAXP = 32
TOK_DEV = 512
VHD = 80
MAXM = 8
IMAGES = 32
TOKENS = 2048
N_TP = 4


def layout_tables(key):
    width_wide = IMAGES // IMG_DEV
    rank_key, owner_key, count_key, shift_key = jax.random.split(jax.random.fold_in(key, 7), 4)
    source_rank = jax.random.permutation(rank_key, width_wide).astype(jnp.int32)
    owner_order = jax.random.permutation(owner_key, width_wide).astype(jnp.int32)
    image_ids = jnp.arange(IMAGES, dtype=jnp.int32)
    source = image_ids // IMG_DEV
    within = image_ids % IMG_DEV
    owner_ids = owner_order[(source_rank[source] + within) % width_wide]
    lowest = max(1, 3 * MAXM // 4)
    merged = jax.random.randint(count_key, (IMAGES,), lowest, MAXM + 1).astype(jnp.int32)
    forced = (source == 0) & (within % width_wide == 0)
    merged = jnp.where(forced, MAXM, merged).astype(jnp.int32)
    slot_rows = TOK_DEV // IMG_DEV
    shift_rows = jax.random.randint(shift_key, (IMAGES,), 0, slot_rows - merged + 1).astype(jnp.int32)
    start_rows = within * slot_rows + shift_rows
    return (merged * 4, jnp.stack([owner_ids, start_rows], axis=1))


def draw_patch_counts(key, part):
    return layout_tables(key)[0].astype(jnp.int32)


def draw_placement(key, part):
    return layout_tables(key)[1].astype(jnp.int32)


def draw_patches(key, part):
    base_key = jax.random.fold_in(jax.random.fold_in(key, 13), 0)
    total_rows = IMAGES * MAXP
    field = jnp.clip(jax.random.normal(base_key, (total_rows, VD), jnp.float32), -4.0, 4.0)
    return field.astype(jnp.bfloat16)


def draw_text_embeds(key, part):
    base_key = jax.random.fold_in(jax.random.fold_in(key, 17), 0)
    field = jnp.clip(jax.random.normal(base_key, (TOKENS, LD), jnp.float32), -4.0, 4.0)
    return field.astype(jnp.bfloat16)


def draw_vit_qkv(key, part):
    base_key = jax.random.fold_in(jax.random.fold_in(key, 11), 0)
    base = jnp.clip(jax.random.normal(base_key, (VD, 3, VD), jnp.float32), -4.0, 4.0) * VD ** (-0.5)
    return base.astype(jnp.bfloat16)


def plant(drawn, rng, low, top_value):
    place = [jax.random.randint(jax.random.fold_in(rng, axis), (), 0, length) for axis, length in enumerate(drawn.shape)]
    widest = drawn.shape.index(max(drawn.shape))
    beside = place[:widest] + [(place[widest] + 1) % drawn.shape[widest]] + place[widest + 1:]
    return drawn.at[tuple(place)].set(low).at[tuple(beside)].set(top_value)


def spiked(result, rng, source, target, parts, factor):
    owner, partner = [(jnp.arange(result.shape[dim]) // (result.shape[dim] // parts)).reshape([-1 if axis == dim else 1 for axis in range(result.ndim)]) for dim in (source, target)]
    chosen = jax.random.permutation(rng, parts)[partner]
    strong = (owner == chosen) | (owner == (partner + parts // 2) % parts)
    return jnp.where(strong, factor * result, result)


def block_levels(stream_key, extent, shards, least, high):
    def one(dim, blocks):
        draws = jax.random.uniform(jax.random.fold_in(jax.random.fold_in(stream_key, 6), dim), (blocks,), jnp.float32, least / len(shards), high / len(shards))
        return jnp.repeat(jnp.exp(draws), extent[dim] // blocks).reshape((-1,) + (1,) * (len(extent) - dim - 1))

    gain = one(*shards[0])
    for cut in shards[1:]:
        gain = gain * one(*cut)
    return gain


def bell_draw(key, extent, scale, most, cuts=(), kind=jnp.bfloat16):
    drawn = scale * jax.random.normal(key, extent, jnp.float32)
    if cuts:
        drawn = drawn * block_levels(key, extent, cuts, -0.22, 0.18)
    return jnp.clip(drawn, -most, most).astype(kind)


def heavy_noise(own_key, dims, scale, bound, shards, heavy, kind=jnp.bfloat16):
    array = scale * jax.random.normal(own_key, dims, jnp.float32)
    if shards:
        array = array * block_levels(own_key, dims, shards, -0.22, 0.18)
    return jnp.clip(spiked(array, jax.random.fold_in(own_key, 3), *heavy), -bound, bound).astype(kind)


def setup_inputs(seed: int = 0, part: int = 0) -> dict:
    keys = jax.random.split(jax.random.key(seed), 16)
    part_splits = jax.random.split(jax.random.fold_in(keys[15], part), 16)
    return {
        "patches": draw_patches(jax.random.fold_in(jax.random.fold_in(keys[15], part), 71), part),
        "patch_counts": draw_patch_counts(jax.random.fold_in(jax.random.fold_in(keys[15], part), 71), part),
        "placement": draw_placement(jax.random.fold_in(jax.random.fold_in(keys[15], part), 71), part),
        "positions": plant(jax.random.randint(part_splits[3], (3, TOKENS), 0, TOKENS), jax.random.fold_in(part_splits[3], 1), 0, TOKENS - 1).astype(jnp.int32),
        "text_embeds": draw_text_embeds(jax.random.fold_in(jax.random.fold_in(keys[15], part), 71), part),
        "vit_gain": jnp.clip(1.0 + 0.18 * jax.random.normal(keys[5], (VD,), jnp.float32), 0.1, 1.9),
        "vit_qkv": draw_vit_qkv(jax.random.fold_in(keys[15], 71), part),
        "vit_proj": bell_draw(keys[7], (VD, VD), VD ** -0.5, 0.15625, ((0, 4),)),
        "merger_gain": jnp.clip(1.0 + 0.18 * jax.random.normal(keys[8], (VD,), jnp.float32), 0.1, 1.9),
        "merger_up": bell_draw(keys[9], (4 * VD, MH), (4 * VD) ** -0.5, 0.078125, ((1, 4),)),
        "merger_down": heavy_noise(keys[10], (MH, LD), MH ** -0.5, 0.15625, ((0, 4),), (0, 1, 4, 2.0)),
        "llm_gain": jnp.clip(1.0 + 0.18 * jax.random.normal(keys[11], (LD,), jnp.float32), 0.1, 1.9),
        "llm_query": bell_draw(keys[12], (LD, QH * HD), LD ** -0.5, 0.0625, ((0, 4), (1, 4))),
        "llm_key": bell_draw(keys[13], (LD, KVH * HD), LD ** -0.5, 0.0625, ((0, 4), (1, 4))),
        "llm_value": bell_draw(keys[14], (LD, KVH * HD), LD ** -0.5, 0.0625, ((0, 4), (1, 4))),
    }


NORM_EPS = 1e-06
ROPE_BASE = 1000000.0

def layer_norm(inputs, scale_gain):
    center = lax.optimization_barrier(jnp.mean(inputs, axis=-1, keepdims=True))
    shifted = inputs - center
    spread = lax.optimization_barrier(jnp.mean(shifted * shifted, axis=-1, keepdims=True))
    return shifted * lax.rsqrt(spread + NORM_EPS) * scale_gain

def rms_norm(inputs, scale_gain):
    square = lax.optimization_barrier(jnp.mean(inputs * inputs, axis=-1, keepdims=True))
    return inputs * lax.rsqrt(square + NORM_EPS) * scale_gain

def rotary(values, positions):
    half_size = HD // 2
    frequency = jnp.arange(half_size).astype(jnp.float32)
    inverse = ROPE_BASE ** (-2.0 * frequency / HD)
    first_end = HD // 8
    second = first_end + 3 * HD // 16
    ordinal = jnp.arange(half_size)
    section = jnp.where(ordinal < first_end, 0, jnp.where(ordinal < second, 1, 2))
    chosen = jnp.where(section[:, None] == 0, positions[0][None, :], jnp.where(section[:, None] == 1, positions[1][None, :], positions[2][None, :]))
    angles = chosen.T.astype(jnp.float32) * inverse[None, :]
    angles = jnp.concatenate([angles, angles], axis=1)
    cosine = jnp.cos(angles)[:, None, :]
    sine_table = jnp.sin(angles)[:, None, :]
    upper_half = values[..., :half_size]
    lower_half = values[..., half_size:]
    turned = jnp.concatenate([-lower_half, upper_half], axis=-1)
    return values * cosine + turned * sine_table

def reference(patches, patch_counts, placement, positions, text_embeds, vit_gain, vit_qkv, vit_proj, merger_gain, merger_up, merger_down, llm_gain, llm_query, llm_key, llm_value):
    patch_rows = patches.astype(jnp.float32)
    normed = layer_norm(patch_rows, vit_gain).astype(jnp.bfloat16)
    triple = jnp.dot(normed, vit_qkv.reshape(VD, 3 * VD), preferred_element_type=jnp.float32)
    triple = lax.optimization_barrier(triple.astype(jnp.bfloat16))
    triple = triple.reshape(IMAGES, MAXP, 3, VH, VHD).astype(jnp.float32)
    scores = jnp.einsum('iqhd,ikhd->ihqk', triple[:, :, 0], triple[:, :, 1]) * VHD ** (-0.5)
    present = jnp.arange(MAXP)[None, :] < patch_counts[:, None]
    scores = jnp.where(present[:, None, None, :], scores, -jnp.inf)
    highest = lax.optimization_barrier(jnp.max(scores, axis=-1, keepdims=True))
    raised = jnp.exp(scores - highest)
    attention_weights = (raised / lax.optimization_barrier(jnp.sum(raised, axis=-1, keepdims=True))).astype(jnp.bfloat16)
    attention_weights = lax.optimization_barrier(attention_weights).astype(jnp.float32)
    context = jnp.einsum('ihqk,ikhd->iqhd', attention_weights, triple[:, :, 2])
    context = context.astype(jnp.bfloat16).reshape(IMAGES * MAXP, VD)
    group_width = VD // N_TP
    attended = jnp.zeros((IMAGES * MAXP, VD), jnp.float32)
    for member in range(N_TP):
        share = jnp.dot(context[:, member * group_width:(member + 1) * group_width], vit_proj[member * group_width:(member + 1) * group_width], preferred_element_type=jnp.float32)
        attended = attended + lax.optimization_barrier(share.astype(jnp.bfloat16)).astype(jnp.float32)
    mixed_rows = patch_rows + attended
    merged_in = layer_norm(mixed_rows, merger_gain).astype(jnp.bfloat16).reshape(IMAGES * MAXM, 4 * VD)
    hidden = jax.nn.gelu(jnp.dot(merged_in, merger_up, preferred_element_type=jnp.float32), approximate=False).astype(jnp.bfloat16)
    unit_width = MH // N_TP
    summed = jnp.zeros((IMAGES * MAXM, LD), jnp.float32)
    for member in range(N_TP):
        share = jnp.dot(hidden[:, member * unit_width:(member + 1) * unit_width], merger_down[member * unit_width:(member + 1) * unit_width], preferred_element_type=jnp.float32)
        summed = summed + lax.optimization_barrier(share.astype(jnp.bfloat16)).astype(jnp.float32)
    visual = summed.astype(jnp.bfloat16)
    merged_count = patch_counts // 4
    offsets = jnp.arange(MAXM).astype(jnp.int32)
    targets = placement[:, 0:1] * TOK_DEV + placement[:, 1:2] + offsets[None, :]
    targets = jnp.where(offsets[None, :] < merged_count[:, None], targets, TOKENS).astype(jnp.int32)
    prompt_rows = text_embeds.at[targets.reshape(-1)].set(visual, mode='drop')
    normed_prompt = rms_norm(prompt_rows.astype(jnp.float32), llm_gain).astype(jnp.bfloat16)
    queries = jnp.dot(normed_prompt, llm_query, preferred_element_type=jnp.float32).reshape(TOKENS, QH, HD)
    queries = rotary(queries, positions).astype(jnp.bfloat16).reshape(TOKENS, QH * HD)
    key_rows = jnp.dot(normed_prompt, llm_key, preferred_element_type=jnp.float32).reshape(TOKENS, KVH, HD)
    key_rows = rotary(key_rows, positions).astype(jnp.bfloat16).reshape(TOKENS, KVH * HD)
    value_rows = jnp.dot(normed_prompt, llm_value, preferred_element_type=jnp.float32).astype(jnp.bfloat16)
    return (queries, key_rows, value_rows)
```

```python
import jax
import jax.numpy as jnp
import numpy as np
from jax import lax
from jax.sharding import PartitionSpec as P

HD = 128
IMG_DEV = 8
MAXP = 32
VHD = 80
MAXM = 8

NORM_EPS = 1e-06
ROPE_BASE = 1000000.0


LINE_BLOCKS = np.array([[0, 1, 2, 3], [1, 0, 2, 3], [2, 3, 1, 0], [3, 2, 1, 0]], np.int32)


def layer_norm(inputs, scale_gain):
    center = jnp.mean(inputs, axis=-1, keepdims=True)
    shifted = inputs - center
    spread = jnp.mean(shifted * shifted, axis=-1, keepdims=True)
    return shifted * lax.rsqrt(spread + NORM_EPS) * scale_gain


def rotary_tables(positions):
    half_size = HD // 2
    frequency = jnp.arange(half_size).astype(jnp.float32)
    inverse = ROPE_BASE ** (-2.0 * frequency / HD)
    first_end = HD // 8
    second = first_end + 3 * HD // 16
    ordinal = jnp.arange(half_size)
    section = jnp.where(ordinal < first_end, 0, jnp.where(ordinal < second, 1, 2))
    chosen = jnp.where(
        section[:, None] == 0,
        positions[0][None, :],
        jnp.where(section[:, None] == 1, positions[1][None, :], positions[2][None, :]),
    )
    angles = chosen.T.astype(jnp.float32) * inverse[None, :]
    return jnp.cos(angles), jnp.sin(angles)


def rotate(values, cosine, sine):
    rows = values.shape[0]
    heads = values.reshape(rows, -1, HD)
    upper = heads[..., : HD // 2]
    lower = heads[..., HD // 2 :]
    cosine = cosine[:, None, :]
    sine = sine[:, None, :]
    turned = jnp.concatenate([upper * cosine - lower * sine, lower * cosine + upper * sine], axis=-1)
    return turned.reshape(rows, -1)


def line_gather(block, size):
    place = lax.axis_index("tp")
    if size != 4:
        whole = lax.all_gather(block, "tp", axis=0)
        return [whole[j] for j in range(size)]
    pair = lax.ppermute(block, "tp", [(0, 1), (1, 0), (2, 3), (3, 2)])
    cross = lax.ppermute(block, "tp", [(1, 2), (2, 1)])
    outer = lax.ppermute(cross, "tp", [(1, 0), (2, 3)])
    cross_far = lax.ppermute(pair, "tp", [(1, 2), (2, 1)])
    outer_far = lax.ppermute(cross_far, "tp", [(1, 0), (2, 3)])
    at_end = (place == 0) | (place == 3)
    return [block, pair, jnp.where(at_end, outer, cross), jnp.where(at_end, outer_far, cross_far)]


def line_order(size):
    place = lax.axis_index("tp")
    if size != 4:
        same = jnp.arange(size, dtype=jnp.int32)
        return same, same
    return (
        jnp.asarray(LINE_BLOCKS)[place],
        jnp.asarray(np.argsort(LINE_BLOCKS, axis=1).astype(np.int32))[place],
    )


def handoff_tables(patch_counts, placement, width_wide, myself, capacity, rows):
    merged_count = patch_counts // 4
    owners = placement[:, 0]
    starts = placement[:, 1]
    owner_grid = owners.reshape(width_wide, IMG_DEV)
    count_grid = merged_count.reshape(width_wide, IMG_DEV)
    ordinal = jnp.arange(IMG_DEV)
    before = ordinal[:, None] < ordinal[None, :]
    same_owner = owner_grid[:, :, None] == owner_grid[:, None, :]
    offsets = jnp.sum(jnp.where(same_owner & before[None], count_grid[:, :, None], 0), axis=1)
    mine_owner = lax.dynamic_index_in_dim(owner_grid, myself, 0, keepdims=False)
    mine_count = lax.dynamic_index_in_dim(count_grid, myself, 0, keepdims=False)
    mine_offset = lax.dynamic_index_in_dim(offsets, myself, 0, keepdims=False)
    target = jnp.arange(width_wide)[:, None, None]
    slot_index = jnp.arange(capacity)[None, :, None]
    matches = (
        (mine_owner[None, None, :] == target)
        & (slot_index >= mine_offset[None, None, :])
        & (slot_index < mine_offset[None, None, :] + mine_count[None, None, :])
    )
    source_row = ordinal[None, None, :] * MAXM + slot_index - mine_offset[None, None, :]
    send_index = jnp.sum(jnp.where(matches, source_row, 0), axis=-1)
    row_place = jnp.arange(rows)[:, None]
    inside = (
        (owners[None, :] == myself)
        & (row_place >= starts[None, :])
        & (row_place < starts[None, :] + merged_count[None, :])
    )
    image_source = jnp.arange(owners.shape[0]) // IMG_DEV
    flat_slot = (
        image_source[None, :] * capacity
        + offsets.reshape(-1)[None, :]
        + row_place
        - starts[None, :]
    )
    take_index = jnp.sum(jnp.where(inside, flat_slot, 0), axis=-1)
    take_live = jnp.any(inside, axis=-1)
    return (send_index, take_index, take_live)


def gather_weights(shard, groups, width_wide):
    depth = shard.shape[0]
    mine = lax.axis_index("wide")
    if groups != 2 or width_wide != 4:
        whole = lax.all_gather(shard, "wide", axis=0)
        return [(j, 0, whole[j]) for j in range(width_wide)]
    half = depth // 2
    group = lax.axis_index("groups")
    core = [(0, 1), (1, 0), (2, 3), (3, 2)]
    part = lax.dynamic_slice_in_dim(shard, group * half, half, 0)
    first = lax.ppermute(part, "wide", [(0, 2), (2, 0), (1, 3), (3, 1)])
    second = lax.ppermute(first, "groups", [(0, 1), (1, 0)])
    beside = lax.ppermute(shard, "wide", core)
    first_beside = lax.ppermute(first, "wide", core)
    second_beside = lax.ppermute(second, "wide", core)
    return [
        (mine, 0, shard),
        (mine ^ 1, 0, beside),
        (mine ^ 2, group * half, first),
        (mine ^ 2, half - group * half, second),
        (mine ^ 3, group * half, first_beside),
        (mine ^ 3, half - group * half, second_beside),
    ]


def project(slots, places, gain, pieces):
    rows, width = slots[0].shape
    stacked = jnp.stack(slots)
    squares = sum(jnp.sum(jnp.square(s.astype(jnp.float32)), axis=-1) for s in slots)
    features = width * len(slots)
    scale = lax.rsqrt(squares / features + NORM_EPS)
    gain_blocks = gain.reshape(len(slots), width)
    total = None
    if len(pieces) == len(slots) or pieces[0][2].shape[0] == width:
        for block, first, weight in pieces:
            depth = weight.shape[0]
            part = lax.dynamic_slice(stacked, (places[block], 0, first), (1, rows, depth))[0]
            scaled = lax.dynamic_slice(gain_blocks, (block, first), (1, depth))
            part = (part.astype(jnp.float32) * scaled).astype(jnp.bfloat16)
            term = jnp.dot(part, weight, preferred_element_type=jnp.float32)
            total = term if total is None else total + term
    else:
        flat = jnp.concatenate([slots[j] for j in range(len(slots))], axis=1)
        flat = (flat.astype(jnp.float32) * gain).astype(jnp.bfloat16)
        weight = jnp.concatenate([p[2] for p in pieces], axis=0)
        total = jnp.dot(flat, weight, preferred_element_type=jnp.float32)
    return total * scale[:, None]


def per_device(
    patches,
    patch_counts,
    placement,
    positions,
    text_embeds,
    vit_gain,
    vit_qkv,
    vit_proj,
    merger_gain,
    merger_up,
    merger_down,
    llm_gain,
    llm_query,
    llm_key,
    llm_value,
):
    groups = lax.axis_size("groups")
    width_wide = lax.axis_size("wide")
    size = lax.axis_size("tp")
    myself = lax.axis_index("wide")
    place = lax.axis_index("tp")
    order, places = line_order(size)
    width = patches.shape[1]
    capacity = MAXM * ((IMG_DEV + width_wide - 1) // width_wide)
    tokens = text_embeds.shape[0]
    local_heads = vit_qkv.shape[2] // VHD
    send_index, take_index, take_live = handoff_tables(
        patch_counts, placement, width_wide, myself, capacity, tokens
    )

    weight_shard = jnp.concatenate([llm_query, llm_key, llm_value], axis=1)
    pieces = gather_weights(weight_shard, groups, width_wide)
    text_slots = line_gather(text_embeds, size)

    patch_rows = patches.astype(jnp.float32)
    normed = layer_norm(patch_rows, vit_gain).astype(jnp.bfloat16)
    triple = jnp.dot(normed, vit_qkv.reshape(width, -1), preferred_element_type=jnp.float32)
    triple = triple.astype(jnp.bfloat16).reshape(IMG_DEV, MAXP, 3, local_heads, VHD)
    scores = jnp.einsum(
        "iqhd,ikhd->ihqk", triple[:, :, 0], triple[:, :, 1], preferred_element_type=jnp.float32
    ) * VHD ** (-0.5)
    own_counts = lax.dynamic_slice_in_dim(patch_counts, myself * IMG_DEV, IMG_DEV)
    present = jnp.arange(MAXP)[None, :] < own_counts[:, None]
    scores = jnp.where(present[:, None, None, :], scores, -jnp.inf)
    highest = jnp.max(scores, axis=-1, keepdims=True)
    raised = jnp.exp(scores - highest)
    probs = (raised / jnp.sum(raised, axis=-1, keepdims=True)).astype(jnp.bfloat16)
    context = jnp.einsum(
        "ihqk,ikhd->iqhd", probs, triple[:, :, 2], preferred_element_type=jnp.float32
    ).astype(jnp.bfloat16)
    context = context.reshape(IMG_DEV * MAXP, local_heads * VHD)
    partial_heads = jnp.dot(context, vit_proj, preferred_element_type=jnp.float32)

    share_rows = IMG_DEV * MAXP // size
    shares = partial_heads.astype(jnp.bfloat16).reshape(size, share_rows, width)
    shares = lax.all_to_all(shares, "tp", split_axis=0, concat_axis=0, tiled=True)
    attended = jnp.sum(shares.astype(jnp.float32), axis=0)
    own_rows = lax.dynamic_slice_in_dim(patch_rows, place * share_rows, share_rows, 0)
    merged_rows = IMG_DEV * MAXM // size
    merged_in = layer_norm(own_rows + attended, merger_gain).astype(jnp.bfloat16)
    merged_in = merged_in.reshape(merged_rows, 4 * width)
    merged_all = jnp.concatenate(line_gather(merged_in, size), axis=0)
    hidden = jax.nn.gelu(
        jnp.dot(merged_all, merger_up, preferred_element_type=jnp.float32), approximate=False
    ).astype(jnp.bfloat16)
    picked = send_index.reshape(-1)
    picked = places[picked // merged_rows] * merged_rows + picked % merged_rows
    packed = jnp.take(hidden, picked, axis=0)
    partial_visual = jnp.dot(packed, merger_down, preferred_element_type=jnp.float32)
    slices = partial_visual.astype(jnp.bfloat16).reshape(width_wide, capacity, size, -1)
    slices = jnp.transpose(slices, (0, 2, 1, 3)).reshape(width_wide * size, capacity, -1)
    slices = lax.all_to_all(slices, ("wide", "tp"), split_axis=0, concat_axis=0, tiled=True)
    visual = jnp.sum(slices.reshape(width_wide, size, capacity, -1).astype(jnp.float32), axis=1)
    visual = visual.astype(jnp.bfloat16).reshape(width_wide * capacity, -1)
    visual_slots = line_gather(visual, size)

    text_out = project(text_slots, places, llm_gain, pieces)
    visual_out = project(visual_slots, places, llm_gain, pieces)
    joined = jnp.where(take_live[:, None], jnp.take(visual_out, take_index, axis=0), text_out)
    cosine, sine = rotary_tables(positions)
    q_end = llm_query.shape[1]
    k_end = q_end + llm_key.shape[1]
    queries = rotate(joined[:, :q_end], cosine, sine).astype(jnp.bfloat16)
    key_rows = rotate(joined[:, q_end:k_end], cosine, sine).astype(jnp.bfloat16)
    value_rows = joined[:, k_end:].astype(jnp.bfloat16)
    return (queries, key_rows, value_rows)


def solution(mesh):
    return jax.shard_map(
        per_device,
        mesh=mesh,
        in_specs=(
            P(("groups", "wide"), None),
            P("groups"),
            P("groups", None),
            P(None, ("groups", "wide")),
            P(("groups", "wide"), "tp"),
            P(),
            P(None, None, "tp"),
            P("tp", None),
            P(),
            P(None, "tp"),
            P("tp", None),
            P(),
            P("wide", "tp"),
            P("wide", "tp"),
            P("wide", "tp"),
        ),
        out_specs=(
            P(("groups", "wide"), "tp"),
            P(("groups", "wide"), "tp"),
            P(("groups", "wide"), "tp"),
        ),
        check_vma=False,
    )
```

```python
import jax
import jax.numpy as jnp
import numpy as np
from jax import lax
from jax.experimental import pallas as pl
from jax.experimental.pallas import tpu as pltpu
from jax.sharding import PartitionSpec as P

HD = 128
IMG_DEV = 8
MAXP = 32
VHD = 80
MAXM = 8

NORM_EPS = 1e-06
ROPE_BASE = 1000000.0


LINE_BLOCKS = np.array([[0, 1, 2, 3], [1, 0, 2, 3], [2, 3, 1, 0], [3, 2, 1, 0]], np.int32)


def layer_norm(inputs, scale_gain):
    center = jnp.mean(inputs, axis=-1, keepdims=True)
    shifted = inputs - center
    spread = jnp.mean(shifted * shifted, axis=-1, keepdims=True)
    return shifted * lax.rsqrt(spread + NORM_EPS) * scale_gain


def rotary_tables(positions):
    half_size = HD // 2
    frequency = jnp.arange(half_size).astype(jnp.float32)
    inverse = ROPE_BASE ** (-2.0 * frequency / HD)
    first_end = HD // 8
    second = first_end + 3 * HD // 16
    ordinal = jnp.arange(half_size)
    section = jnp.where(ordinal < first_end, 0, jnp.where(ordinal < second, 1, 2))
    chosen = jnp.where(
        section[:, None] == 0,
        positions[0][None, :],
        jnp.where(section[:, None] == 1, positions[1][None, :], positions[2][None, :]),
    )
    angles = chosen.T.astype(jnp.float32) * inverse[None, :]
    return jnp.cos(angles), jnp.sin(angles)


def rotate(values, cosine, sine):
    rows = values.shape[0]
    heads = values.reshape(rows, -1, HD)
    upper = heads[..., : HD // 2]
    lower = heads[..., HD // 2 :]
    cosine = cosine[:, None, :]
    sine = sine[:, None, :]
    turned = jnp.concatenate([upper * cosine - lower * sine, lower * cosine + upper * sine], axis=-1)
    return turned.reshape(rows, -1)


def line_gather(block, size):
    place = lax.axis_index("tp")
    if size != 4:
        whole = lax.all_gather(block, "tp", axis=0)
        return [whole[j] for j in range(size)]
    pair = lax.ppermute(block, "tp", [(0, 1), (1, 0), (2, 3), (3, 2)])
    cross = lax.ppermute(block, "tp", [(1, 2), (2, 1)])
    outer = lax.ppermute(cross, "tp", [(1, 0), (2, 3)])
    cross_far = lax.ppermute(pair, "tp", [(1, 2), (2, 1)])
    outer_far = lax.ppermute(cross_far, "tp", [(1, 0), (2, 3)])
    at_end = (place == 0) | (place == 3)
    return [block, pair, jnp.where(at_end, outer, cross), jnp.where(at_end, outer_far, cross_far)]


def line_order(size):
    place = lax.axis_index("tp")
    if size != 4:
        same = jnp.arange(size, dtype=jnp.int32)
        return same, same
    return (
        jnp.asarray(LINE_BLOCKS)[place],
        jnp.asarray(np.argsort(LINE_BLOCKS, axis=1).astype(np.int32))[place],
    )


def handoff_tables(patch_counts, placement, width_wide, myself, capacity, rows):
    merged_count = patch_counts // 4
    owners = placement[:, 0]
    starts = placement[:, 1]
    owner_grid = owners.reshape(width_wide, IMG_DEV)
    count_grid = merged_count.reshape(width_wide, IMG_DEV)
    ordinal = jnp.arange(IMG_DEV)
    before = ordinal[:, None] < ordinal[None, :]
    same_owner = owner_grid[:, :, None] == owner_grid[:, None, :]
    offsets = jnp.sum(jnp.where(same_owner & before[None], count_grid[:, :, None], 0), axis=1)
    mine_owner = lax.dynamic_index_in_dim(owner_grid, myself, 0, keepdims=False)
    mine_count = lax.dynamic_index_in_dim(count_grid, myself, 0, keepdims=False)
    mine_offset = lax.dynamic_index_in_dim(offsets, myself, 0, keepdims=False)
    target = jnp.arange(width_wide)[:, None, None]
    slot_index = jnp.arange(capacity)[None, :, None]
    matches = (
        (mine_owner[None, None, :] == target)
        & (slot_index >= mine_offset[None, None, :])
        & (slot_index < mine_offset[None, None, :] + mine_count[None, None, :])
    )
    source_row = ordinal[None, None, :] * MAXM + slot_index - mine_offset[None, None, :]
    send_index = jnp.sum(jnp.where(matches, source_row, 0), axis=-1)
    row_place = jnp.arange(rows)[:, None]
    inside = (
        (owners[None, :] == myself)
        & (row_place >= starts[None, :])
        & (row_place < starts[None, :] + merged_count[None, :])
    )
    image_source = jnp.arange(owners.shape[0]) // IMG_DEV
    flat_slot = (
        image_source[None, :] * capacity
        + offsets.reshape(-1)[None, :]
        + row_place
        - starts[None, :]
    )
    take_index = jnp.sum(jnp.where(inside, flat_slot, 0), axis=-1)
    take_live = jnp.any(inside, axis=-1)
    return (send_index, take_index, take_live)


def gather_weights(shard, groups, width_wide):
    depth = shard.shape[0]
    mine = lax.axis_index("wide")
    if groups != 2 or width_wide != 4:
        whole = lax.all_gather(shard, "wide", axis=0)
        return [(j, 0, whole[j]) for j in range(width_wide)]
    half = depth // 2
    group = lax.axis_index("groups")
    core = [(0, 1), (1, 0), (2, 3), (3, 2)]
    part = lax.dynamic_slice_in_dim(shard, group * half, half, 0)
    first = lax.ppermute(part, "wide", [(0, 2), (2, 0), (1, 3), (3, 1)])
    second = lax.ppermute(first, "groups", [(0, 1), (1, 0)])
    beside = lax.ppermute(shard, "wide", core)
    first_beside = lax.ppermute(first, "wide", core)
    second_beside = lax.ppermute(second, "wide", core)
    return [
        (mine, 0, shard),
        (mine ^ 1, 0, beside),
        (mine ^ 2, group * half, first),
        (mine ^ 2, half - group * half, second),
        (mine ^ 3, group * half, first_beside),
        (mine ^ 3, half - group * half, second_beside),
    ]


def project(slots, places, gain, pieces):
    rows, width = slots[0].shape
    stacked = jnp.stack(slots)
    squares = sum(jnp.sum(jnp.square(s.astype(jnp.float32)), axis=-1) for s in slots)
    features = width * len(slots)
    scale = lax.rsqrt(squares / features + NORM_EPS)
    gain_blocks = gain.reshape(len(slots), width)
    total = None
    if len(pieces) == len(slots) or pieces[0][2].shape[0] == width:
        for block, first, weight in pieces:
            depth = weight.shape[0]
            part = lax.dynamic_slice(stacked, (places[block], 0, first), (1, rows, depth))[0]
            scaled = lax.dynamic_slice(gain_blocks, (block, first), (1, depth))
            part = (part.astype(jnp.float32) * scaled).astype(jnp.bfloat16)
            term = jnp.dot(part, weight, preferred_element_type=jnp.float32)
            total = term if total is None else total + term
    else:
        flat = jnp.concatenate([slots[j] for j in range(len(slots))], axis=1)
        flat = (flat.astype(jnp.float32) * gain).astype(jnp.bfloat16)
        weight = jnp.concatenate([p[2] for p in pieces], axis=0)
        total = jnp.dot(flat, weight, preferred_element_type=jnp.float32)
    return total * scale[:, None]


def per_device_any(
    patches,
    patch_counts,
    placement,
    positions,
    text_embeds,
    vit_gain,
    vit_qkv,
    vit_proj,
    merger_gain,
    merger_up,
    merger_down,
    llm_gain,
    llm_query,
    llm_key,
    llm_value,
):
    groups = lax.axis_size("groups")
    width_wide = lax.axis_size("wide")
    size = lax.axis_size("tp")
    myself = lax.axis_index("wide")
    place = lax.axis_index("tp")
    _, places = line_order(size)
    width = patches.shape[1]
    capacity = MAXM * ((IMG_DEV + width_wide - 1) // width_wide)
    tokens = text_embeds.shape[0]
    local_heads = vit_qkv.shape[2] // VHD
    send_index, take_index, take_live = handoff_tables(
        patch_counts, placement, width_wide, myself, capacity, tokens
    )

    weight_shard = jnp.concatenate([llm_query, llm_key, llm_value], axis=1)
    pieces = gather_weights(weight_shard, groups, width_wide)
    text_slots = line_gather(text_embeds, size)

    patch_rows = patches.astype(jnp.float32)
    normed = layer_norm(patch_rows, vit_gain).astype(jnp.bfloat16)
    triple = jnp.dot(normed, vit_qkv.reshape(width, -1), preferred_element_type=jnp.float32)
    triple = triple.astype(jnp.bfloat16).reshape(IMG_DEV, MAXP, 3, local_heads, VHD)
    scores = jnp.einsum(
        "iqhd,ikhd->ihqk", triple[:, :, 0], triple[:, :, 1], preferred_element_type=jnp.float32
    ) * VHD ** (-0.5)
    own_counts = lax.dynamic_slice_in_dim(patch_counts, myself * IMG_DEV, IMG_DEV)
    present = jnp.arange(MAXP)[None, :] < own_counts[:, None]
    scores = jnp.where(present[:, None, None, :], scores, -jnp.inf)
    highest = jnp.max(scores, axis=-1, keepdims=True)
    raised = jnp.exp(scores - highest)
    probs = (raised / jnp.sum(raised, axis=-1, keepdims=True)).astype(jnp.bfloat16)
    context = jnp.einsum(
        "ihqk,ikhd->iqhd", probs, triple[:, :, 2], preferred_element_type=jnp.float32
    ).astype(jnp.bfloat16)
    context = context.reshape(IMG_DEV * MAXP, local_heads * VHD)
    partial_heads = jnp.dot(context, vit_proj, preferred_element_type=jnp.float32)

    share_rows = IMG_DEV * MAXP // size
    shares = partial_heads.astype(jnp.bfloat16).reshape(size, share_rows, width)
    shares = lax.all_to_all(shares, "tp", split_axis=0, concat_axis=0, tiled=True)
    attended = jnp.sum(shares.astype(jnp.float32), axis=0)
    own_rows = lax.dynamic_slice_in_dim(patch_rows, place * share_rows, share_rows, 0)
    merged_rows = IMG_DEV * MAXM // size
    merged_in = layer_norm(own_rows + attended, merger_gain).astype(jnp.bfloat16)
    merged_in = merged_in.reshape(merged_rows, 4 * width)
    merged_all = jnp.concatenate(line_gather(merged_in, size), axis=0)
    hidden = jax.nn.gelu(
        jnp.dot(merged_all, merger_up, preferred_element_type=jnp.float32), approximate=False
    ).astype(jnp.bfloat16)
    picked = send_index.reshape(-1)
    picked = places[picked // merged_rows] * merged_rows + picked % merged_rows
    packed = jnp.take(hidden, picked, axis=0)
    partial_visual = jnp.dot(packed, merger_down, preferred_element_type=jnp.float32)
    slices = partial_visual.astype(jnp.bfloat16).reshape(width_wide, capacity, size, -1)
    slices = jnp.transpose(slices, (0, 2, 1, 3)).reshape(width_wide * size, capacity, -1)
    slices = lax.all_to_all(slices, ("wide", "tp"), split_axis=0, concat_axis=0, tiled=True)
    visual = jnp.sum(slices.reshape(width_wide, size, capacity, -1).astype(jnp.float32), axis=1)
    visual = visual.astype(jnp.bfloat16).reshape(width_wide * capacity, -1)
    visual_slots = line_gather(visual, size)

    text_out = project(text_slots, places, llm_gain, pieces)
    visual_out = project(visual_slots, places, llm_gain, pieces)
    joined = jnp.where(take_live[:, None], jnp.take(visual_out, take_index, axis=0), text_out)
    cosine, sine = rotary_tables(positions)
    q_end = llm_query.shape[1]
    k_end = q_end + llm_key.shape[1]
    queries = rotate(joined[:, :q_end], cosine, sine).astype(jnp.bfloat16)
    key_rows = rotate(joined[:, q_end:k_end], cosine, sine).astype(jnp.bfloat16)
    value_rows = joined[:, k_end:].astype(jnp.bfloat16)
    return (queries, key_rows, value_rows)


def named_exchange(value, axes):
    return lax.all_to_all(value, axes, split_axis=0, concat_axis=0, tiled=True)


ENDS = [(0, 1), (1, 0), (2, 3), (3, 2)]
MIDDLE = [(1, 2), (2, 1)]
OUTWARD = [(1, 0), (2, 3)]
ACROSS = [(0, 2), (2, 0), (1, 3), (3, 1)]
MINP = 24
TILE = 256
PIECES = 2


def fetch_weights(state, slot, weights, buffer, sems, tiles):
    own, beside = weights[0:3], weights[3:6]
    far = weights[6 : 6 + 2 * PIECES]
    far_beside = weights[6 + 2 * PIECES :]
    where, group = state[slot], state[8]
    piece = far[0].shape[0]
    q_tiles = own[0].shape[1] // TILE
    for tile in range(tiles):
        columns = pl.ds(tile * TILE, TILE)
        for which, parts in ((0, own), (1, beside)):
            source = parts[0].at[:, columns] if tile < q_tiles else parts[1 + tile - q_tiles]

            @pl.when(where == which)
            def _():
                pltpu.make_async_copy(source, buffer.at[:, columns], sems.at[tile]).start()

        for which, parts in ((2, far), (3, far_beside)):

            @pl.when(where == which)
            def _():
                for rank in range(2):
                    for index in range(PIECES):
                        start = jnp.where(group == rank, 0, PIECES * piece) + index * piece
                        start = pl.multiple_of(start, piece)
                        pltpu.make_async_copy(
                            parts[rank * PIECES + index].at[:, columns],
                            buffer.at[pl.ds(start, piece), columns],
                            sems.at[tile],
                        ).start()


def compact_body(myself, counts, placement, text, gain, out_a, out_b, squares, partial):
    tokens, depth = text.shape
    images = counts.shape[1]
    kept = out_a.shape[0] + out_b.shape[0]
    eye = lax.broadcasted_iota(jnp.int32, (images, images), 0) == lax.broadcasted_iota(
        jnp.int32, (images, images), 1
    )
    as_row = lambda col: jnp.sum(jnp.where(eye, col, 0.0), axis=0, keepdims=True)
    as_col = lambda row: jnp.sum(jnp.where(eye, row, 0.0), axis=1, keepdims=True)
    merged = (counts[...] // 4).astype(jnp.float32)
    spots = placement[...].astype(jnp.float32)
    mine_col = (spots[:, 0:1] == myself[0].astype(jnp.float32)).astype(jnp.float32)
    start_col = spots[:, 1:2]
    count_row = merged * as_row(mine_col)
    count_col = as_col(merged) * mine_col
    start_row = as_row(start_col)
    earlier = jnp.sum(jnp.where(start_col < start_row, count_col, 0.0), axis=0, keepdims=True)
    threshold = start_row - earlier
    order = lax.broadcasted_iota(jnp.int32, (kept, images), 0).astype(jnp.float32)
    rows = jnp.sum(jnp.where(order >= threshold, count_row, 0.0), axis=1, keepdims=True)
    rows = jnp.minimum(rows + order[:, 0:1], tokens - 1.0)
    lanes = lax.broadcasted_iota(jnp.int32, (kept, tokens), 1).astype(jnp.float32)
    select = (lanes == rows).astype(jnp.float32).astype(jnp.bfloat16)
    low = 0
    for out in (out_a, out_b):
        high = low + out.shape[0]
        for start in range(0, depth, TILE):
            columns = slice(start, start + TILE)
            chosen = jnp.dot(select[low:high], text[:, columns], preferred_element_type=jnp.float32)
            square = chosen * chosen
            square = sum(square[:, lane : lane + 128] for lane in range(0, TILE, 128))
            if start:
                square = square + partial[low:high, :]
            partial[low:high, :] = square
            out[:, columns] = (chosen * gain[:, columns]).astype(jnp.bfloat16)
        low = high
    totals = lax.dot_general(
        jnp.ones((8, 128), jnp.float32),
        partial[...],
        (((1,), (1,)), ((), ())),
        precision=lax.Precision.HIGHEST,
        preferred_element_type=jnp.float32,
    )
    lines = []
    for start in range(0, kept, 128):
        line = totals[0:1, start : start + 128]
        if line.shape[1] < 128:
            line = jnp.concatenate([line, jnp.zeros((1, 128 - line.shape[1]), jnp.float32)], axis=1)
        lines.append(line)
    coarse = [line.astype(jnp.bfloat16).astype(jnp.float32) for line in lines]
    lines = coarse + [line - near for line, near in zip(lines, coarse)]
    lines.append(jnp.zeros((squares.shape[0] - len(lines), 128), jnp.float32))
    squares[...] = jnp.concatenate(lines, axis=0).astype(jnp.bfloat16)


def compact_call(myself, counts, placement, text, gain, rows, lines):
    whole = lambda x: pl.BlockSpec(x.shape, lambda i: (0,) * len(x.shape))
    tokens, depth = text.shape
    out = (
        jax.ShapeDtypeStruct((rows[0], depth), jnp.bfloat16),
        jax.ShapeDtypeStruct((rows[1], depth), jnp.bfloat16),
        jax.ShapeDtypeStruct((lines, 128), jnp.bfloat16),
    )
    inputs = (counts, placement, text, gain)
    return pl.pallas_call(
        compact_body,
        grid=(1,),
        out_shape=out,
        in_specs=[pl.BlockSpec(memory_space=pltpu.SMEM)] + [whole(x) for x in inputs],
        out_specs=tuple(whole(x) for x in out),
        scratch_shapes=[pltpu.VMEM((sum(rows), 128), jnp.float32)],
        cost_estimate=pl.CostEstimate(
            flops=2 * tokens * sum(rows) * depth, bytes_accessed=4 * tokens * depth, transcendentals=0
        ),
    )(myself, *inputs)


def rope_rows(total, scale, cosine, sine, q_columns, k_columns, result):
    factor = scale[...]
    cos, sin = cosine[...], sine[...]
    columns = total.shape[1]
    for low in range(0, columns, HD):
        values = total[:, low : low + HD] * factor
        if low < q_columns + k_columns:
            values = values * cos + pltpu.roll(values, HD // 2, 1) * sin
        result[:, low : low + HD] = values.astype(jnp.bfloat16)


def load_rows(state, candidates, rows, scaled, sem):
    for index, parts in enumerate(candidates):
        low = 0
        for part, count in zip(parts, rows):
            copy = pltpu.make_async_copy(part, scaled.at[pl.ds(low, count), :], sem)
            if len(candidates) == 1:
                copy.start()
            else:
                pl.when(state[9] == 1 - index)(copy.start)
            low += count


def matmul_slot(slot, scaled, buffer, sems, total, before, tiles):
    now = slot % 2

    def multiply(tile, carry):
        columns = pl.ds(pl.multiple_of(tile * TILE, TILE), TILE)
        target = buffer.at[now, :, columns]
        pltpu.make_async_copy(target, target, sems.at[now, tile]).wait()
        term = jnp.dot(scaled[...], buffer[now, :, columns], preferred_element_type=jnp.float32)
        if before is not None:
            term = term + before[:, columns]
        total[:, columns] = term
        return carry

    lax.fori_loop(0, tiles, multiply, 0)


def text_body(plan, *refs):
    refs = list(refs)
    take = lambda count: [refs.pop(0) for _ in range(count)]
    (state,) = take(1)
    rows = plan["rows"]
    texts = [[take(len(rows)) for _ in range(count)] for count in plan["candidates"]]
    weights = take(6 + 4 * PIECES)
    before = take(1)[0] if plan["has_sum"] else None
    finish = plan["finish"]
    if finish:
        scale, cosine, sine = take(3)
    if finish == 1:
        (ready,) = take(1)
    elif finish == 2:
        groups = take(2)
        places = take(3)
        results = take(3)
    else:
        outputs = take(len(rows))
    scaled, load_sems, buffer, sems, total = take(5)
    if finish == 2:
        (turned,) = take(1)
    tiles = plan["tiles"]
    slots = len(texts)
    fetch_weights(state, 0, weights, buffer.at[0], sems.at[0], tiles)
    load_rows(state, texts[0], rows, scaled.at[0], load_sems.at[0])
    for slot in range(slots):
        now, after = slot % 2, (slot + 1) % 2
        if slot + 1 < slots:
            fetch_weights(state, slot + 1, weights, buffer.at[after], sems.at[after], tiles)
            load_rows(state, texts[slot + 1], rows, scaled.at[after], load_sems.at[after])
        pltpu.make_async_copy(scaled.at[now], scaled.at[now], load_sems.at[now]).wait()
        matmul_slot(slot, scaled.at[now], buffer, sems, total, total if slot else before, tiles)

    q_columns, k_columns = plan["heads"]
    if not finish:
        low = 0
        for out, count in zip(outputs, rows):
            out[...] = total[low : low + count, :]
            low += count
    elif finish == 1:
        rope_rows(total, scale, cosine, sine, q_columns, k_columns, ready)
    else:
        rope_rows(total, scale, cosine, sine, q_columns, k_columns, turned)
        parts = (groups[0], turned, groups[1])
        for low in range(0, total.shape[1], TILE):
            placed = None
            for place, group in zip(places, parts):
                term = jnp.dot(
                    place[...], group[:, low : low + TILE], preferred_element_type=jnp.float32
                )
                placed = term if placed is None else placed + term
            placed = placed.astype(jnp.bfloat16)
            if low < q_columns:
                results[0][:, low : low + TILE] = placed
            elif low < q_columns + k_columns:
                results[1][:, low - q_columns : low - q_columns + TILE] = placed
            else:
                start = low - q_columns - k_columns
                results[2][:, start : start + TILE] = placed


def visual_body(plan, *refs):
    refs = list(refs)
    take = lambda count: [refs.pop(0) for _ in range(count)]
    state, visual, gain = take(3)
    weights = take(6 + 4 * PIECES)
    cosine, sine, ready, scaled, buffer, sems, total = take(7)
    tiles = plan["tiles"]
    blocks, rows, depth = visual.shape
    fetch_weights(state, 0, weights, buffer.at[0], sems.at[0], tiles)
    squares = jnp.zeros((rows, 1), jnp.float32)
    for block in range(blocks):
        text = visual[block].astype(jnp.float32)
        squares = squares + jnp.sum(text * text, axis=-1, keepdims=True)
        scaled[block] = (text * gain[block : block + 1, :]).astype(jnp.bfloat16)
    for slot in range(blocks):
        if slot + 1 < blocks:
            after = (slot + 1) % 2
            fetch_weights(state, slot + 1, weights, buffer.at[after], sems.at[after], tiles)
        matmul_slot(slot, scaled.at[slot], buffer, sems, total, total if slot else None, tiles)
    scale = lax.rsqrt(squares / (blocks * depth) + NORM_EPS)
    rope_rows(total, scale, cosine, sine, *plan["heads"], ready)


def product_call(
    state, texts, weights, rows, visual=None, before=None, finish=0, extra=(), out=(), limit=40
):
    heads = (weights[0].shape[1], weights[1].shape[1])
    columns = sum(heads) + weights[2].shape[1]
    depth = weights[0].shape[0]
    tiles = columns // TILE
    every = sum(rows)
    whole = lambda x: pl.BlockSpec(x.shape, lambda i: (0,) * len(x.shape))
    anywhere = pl.BlockSpec(memory_space=pl.ANY)
    plan = dict(rows=rows, has_sum=before is not None, finish=finish, tiles=tiles, heads=heads)
    late = [*(() if before is None else (before,)), *extra]
    if visual is None:
        slots = len(texts)
        plan["candidates"] = [len(t) for t in texts]
        flat = [part for slot in texts for candidate in slot for part in candidate]
        specs = [anywhere] * len(flat)
        function = text_body
        loads = [pltpu.VMEM((2, every, depth), jnp.bfloat16), pltpu.SemaphoreType.DMA((2,))]
    else:
        slots = visual[0].shape[0]
        flat = list(visual)
        specs = [whole(x) for x in flat]
        function = visual_body
        loads = [pltpu.VMEM((slots, every, depth), jnp.bfloat16)]
    specs = [pl.BlockSpec(memory_space=pltpu.SMEM)] + specs
    specs += [anywhere] * len(weights) + [whole(x) for x in late]
    depth_of = min(2, slots)
    scratch = loads + [
        pltpu.VMEM((depth_of, depth, columns), jnp.bfloat16),
        pltpu.SemaphoreType.DMA((depth_of, tiles)),
        pltpu.VMEM((every, columns), jnp.float32),
    ]
    if finish == 2:
        scratch.append(pltpu.VMEM((every, columns), jnp.bfloat16))
    if not out:
        out = tuple(jax.ShapeDtypeStruct((count, columns), jnp.float32) for count in rows)

    def body(*refs):
        function(plan, *refs)

    return pl.pallas_call(
        body,
        grid=(1,),
        out_shape=out,
        in_specs=specs,
        out_specs=tuple(whole(x) for x in out),
        scratch_shapes=scratch,
        compiler_params=pltpu.CompilerParams(vmem_limit_bytes=limit << 20),
        cost_estimate=pl.CostEstimate(
            flops=2 * every * depth * columns * slots,
            bytes_accessed=2 * depth * columns * slots,
            transcendentals=0,
        ),
    )(state, *flat, *weights, *late)


def text_columns(patch_counts, placement, myself, tokens):
    counts = jnp.where(placement[:, 0] == myself, patch_counts // 4, 0)
    starts = placement[:, 1]
    place = jnp.arange(tokens)
    return place - jnp.sum(jnp.where(place[:, None] >= starts[None, :], counts[None, :], 0), axis=1)


def per_device(
    patches,
    patch_counts,
    placement,
    positions,
    text_embeds,
    vit_gain,
    vit_qkv,
    vit_proj,
    merger_gain,
    merger_up,
    merger_down,
    llm_gain,
    llm_query,
    llm_key,
    llm_value,
):
    width_wide = lax.axis_size("wide")
    size = lax.axis_size("tp")
    myself = lax.axis_index("wide")
    place = lax.axis_index("tp")
    side = lax.axis_index("groups")
    width = patches.shape[1]
    capacity = MAXM * ((IMG_DEV + width_wide - 1) // width_wide)
    tokens, depth = text_embeds.shape
    local_heads = vit_qkv.shape[2] // VHD
    send_index, take_index, take_live = handoff_tables(
        patch_counts, placement, width_wide, myself, capacity, tokens
    )

    blocks = jnp.asarray(LINE_BLOCKS)[place]
    gain_blocks = llm_gain.reshape(size, depth)
    kept = tokens - IMG_DEV * (MINP // 4)
    rows_a = (kept // 2 + 15) // 16 * 16
    rows = [rows_a, kept - rows_a]
    text_a, text_b, squares = compact_call(
        myself.reshape(1),
        patch_counts.reshape(1, -1),
        placement,
        text_embeds,
        lax.dynamic_slice_in_dim(gain_blocks, place, 1, 0),
        rows,
        IMG_DEV * MAXM // size,
    )
    near_a = lax.ppermute(text_a, "tp", ENDS)
    middle_a = lax.ppermute(text_a, "tp", MIDDLE)

    patch_rows = patches.astype(jnp.float32)
    normed = layer_norm(patch_rows, vit_gain).astype(jnp.bfloat16)
    triple = jnp.dot(normed, vit_qkv.reshape(width, -1), preferred_element_type=jnp.float32)
    triple = triple.astype(jnp.bfloat16).reshape(IMG_DEV, MAXP, 3, local_heads, VHD)
    scores = jnp.einsum(
        "iqhd,ikhd->ihqk", triple[:, :, 0], triple[:, :, 1], preferred_element_type=jnp.float32
    ) * VHD ** (-0.5)
    own_counts = lax.dynamic_slice_in_dim(patch_counts, myself * IMG_DEV, IMG_DEV)
    present = jnp.arange(MAXP)[None, :] < own_counts[:, None]
    scores = jnp.where(present[:, None, None, :], scores, -jnp.inf)
    highest = jnp.max(scores, axis=-1, keepdims=True)
    raised = jnp.exp(scores - highest)
    probs = (raised / jnp.sum(raised, axis=-1, keepdims=True)).astype(jnp.bfloat16)
    context = jnp.einsum(
        "ihqk,ikhd->iqhd", probs, triple[:, :, 2], preferred_element_type=jnp.float32
    ).astype(jnp.bfloat16)
    context = context.reshape(IMG_DEV * MAXP, local_heads * VHD)
    partial_heads = jnp.dot(context, vit_proj, preferred_element_type=jnp.float32)

    share_rows = IMG_DEV * MAXP // size
    shares = partial_heads.astype(jnp.bfloat16).reshape(size, share_rows, width)
    shares = named_exchange(shares, "tp")
    near_b = lax.ppermute(text_b, "tp", ENDS)
    middle_b = lax.ppermute(text_b, "tp", MIDDLE)
    piece = depth // (2 * PIECES)
    first, second, first_beside, second_beside = [], [], [], []
    for index in range(PIECES):
        part = jnp.concatenate(
            [
                lax.dynamic_slice_in_dim(w, (side * PIECES + index) * piece, piece, 0)
                for w in (llm_query, llm_key, llm_value)
            ],
            axis=1,
        )
        first.append(lax.ppermute(part, "wide", ACROSS))
        second.append(lax.ppermute(first[index], "groups", [(0, 1), (1, 0)]))
        first_beside.append(lax.ppermute(first[index], "wide", ENDS))
        second_beside.append(lax.ppermute(second[index], "wide", ENDS))
    beside = [lax.ppermute(w, "wide", ENDS) for w in (llm_query, llm_key, llm_value)]
    weights = [llm_query, llm_key, llm_value, *beside]
    weights += [*first, *second, *first_beside, *second_beside]
    attended = jnp.sum(shares.astype(jnp.float32), axis=0)
    own_rows = lax.dynamic_slice_in_dim(patch_rows, place * share_rows, share_rows, 0)
    merged_rows = IMG_DEV * MAXM // size
    merged_in = layer_norm(own_rows + attended, merger_gain).astype(jnp.bfloat16)
    merged_in = merged_in.reshape(merged_rows, 4 * width)
    merged_in = jnp.concatenate([merged_in, squares], axis=1)[None]
    merged_all = named_exchange(jnp.broadcast_to(merged_in, (size,) + merged_in.shape[1:]), "tp")
    squares = merged_all[:, : 2 * ((kept + 127) // 128), 4 * width :].astype(jnp.float32)
    squares = jnp.sum(squares.reshape(2 * size, -1), axis=0)[:kept]
    text_scale = lax.rsqrt(squares / (size * depth) + NORM_EPS)[:, None]
    merged_all = merged_all[:, :, : 4 * width].reshape(size * merged_rows, 4 * width)
    outer_a = lax.ppermute(middle_a, "tp", OUTWARD)
    far_a = lax.ppermute(near_a, "tp", MIDDLE)
    hidden = jax.nn.gelu(
        jnp.dot(merged_all, merger_up, preferred_element_type=jnp.float32), approximate=False
    ).astype(jnp.bfloat16)
    packed = jnp.take(hidden, send_index.reshape(-1), axis=0)
    partial_visual = jnp.dot(packed, merger_down, preferred_element_type=jnp.float32)
    slices = partial_visual.astype(jnp.bfloat16).reshape(width_wide, capacity, size, -1)
    slices = jnp.transpose(slices, (0, 2, 1, 3)).reshape(width_wide * size, capacity, -1)
    slices = named_exchange(slices, ("wide", "tp"))
    outer_b = lax.ppermute(middle_b, "tp", OUTWARD)
    far_b = lax.ppermute(near_b, "tp", MIDDLE)
    visual = jnp.sum(slices.reshape(width_wide, size, capacity, -1).astype(jnp.float32), axis=1)
    visual = visual.astype(jnp.bfloat16).reshape(1, width_wide * capacity, -1)
    visual_all = named_exchange(jnp.broadcast_to(visual, (size,) + visual.shape[1:]), "tp")
    last_a = lax.ppermute(far_a, "tp", OUTWARD)
    last_b = lax.ppermute(far_b, "tp", OUTWARD)

    slots = width_wide * capacity
    back = text_columns(patch_counts, placement, myself, tokens)
    column = jnp.where(take_live, kept + take_index, back)
    select = column[:, None] == jnp.arange(kept + slots)[None, :]
    places = select.astype(jnp.bfloat16)
    places = [places[:, : rows[0]], places[:, rows[0] : kept], places[:, kept:]]
    spots = jnp.sum(jnp.where(select[None], positions[:, :, None], 0), axis=1)
    cosine, sine = rotary_tables(spots)
    cosine = jnp.concatenate([cosine, cosine], axis=1)
    sine = jnp.concatenate([-sine, sine], axis=1)
    cuts = [(0, rows[0]), (rows[0], kept), (kept, kept + slots)]
    cosines = [cosine[low:high] for low, high in cuts]
    sines = [sine[low:high] for low, high in cuts]

    at_end = ((place == 0) | (place == size - 1)).astype(jnp.int32)

    def state_of(chosen):
        chosen = jnp.concatenate([chosen, jnp.zeros((4 - chosen.shape[0],), jnp.int32)])
        rest = jnp.stack([side, at_end, jnp.int32(size * depth)])
        return jnp.concatenate([myself ^ chosen, chosen, rest]).astype(jnp.int32)

    every = jnp.arange(size, dtype=jnp.int32)
    q_columns, k_columns, v_columns = (w.shape[1] for w in weights[:3])
    columns = q_columns + k_columns + v_columns
    early = [[[text_a, text_b]], [[near_a, near_b]], [[outer_a, outer_b], [middle_a, middle_b]]]
    sum_a, sum_b = product_call(state_of(blocks[:3]), early, weights, rows)
    bf16 = lambda *shape: jax.ShapeDtypeStruct(shape, jnp.bfloat16)
    (ready_seen,) = product_call(
        state_of(every), None, weights, [slots], visual=(visual_all, gain_blocks),
        extra=(cosines[2], sines[2]), out=(bf16(slots, columns),),
    )
    last = state_of(blocks[3:])
    (ready_a,) = product_call(
        last, [[[last_a], [far_a]]], weights, rows[:1], before=sum_a, finish=1,
        extra=(text_scale[: rows[0]], cosines[0], sines[0]), out=(bf16(rows[0], columns),),
    )
    return product_call(
        last, [[[last_b], [far_b]]], weights, rows[1:], before=sum_b, finish=2,
        extra=(text_scale[rows[0] :], cosines[1], sines[1], ready_a, ready_seen, *places),
        out=(bf16(tokens, q_columns), bf16(tokens, k_columns), bf16(tokens, v_columns)),
    )


def solution(mesh):
    shape = mesh.shape
    quick = shape["groups"] == 2 and shape["wide"] == 4 and shape["tp"] == 4
    return jax.shard_map(
        per_device if quick else per_device_any,
        mesh=mesh,
        in_specs=(
            P(("groups", "wide"), None),
            P("groups"),
            P("groups", None),
            P(None, ("groups", "wide")),
            P(("groups", "wide"), "tp"),
            P(),
            P(None, None, "tp"),
            P("tp", None),
            P(),
            P(None, "tp"),
            P("tp", None),
            P(),
            P("wide", "tp"),
            P("wide", "tp"),
            P("wide", "tp"),
        ),
        out_specs=(
            P(("groups", "wide"), "tp"),
            P(("groups", "wide"), "tp"),
            P(("groups", "wide"), "tp"),
        ),
        check_vma=False,
    )
```

```python
from types import SimpleNamespace

import jax
import jax.numpy as jnp
import numpy as np
from jax import lax
from jax.experimental import pallas as pl
from jax.experimental.pallas import tpu as pltpu
from jax.sharding import PartitionSpec as P

TP = "tp"
WIDE = "wide"
GROUPS = "groups"
HD = 128
IMG_DEV = 8
MAXP = 32
VHD = 80
MAXM = 8

NORM_EPS = 1e-06
ROPE_BASE = 1000000.0


LINE_BLOCKS = np.array([[0, 1, 2, 3], [1, 0, 2, 3], [2, 3, 1, 0], [3, 2, 1, 0]], np.int32)


def layer_norm(inputs, scale_gain):
    center = jnp.mean(inputs, axis=-1, keepdims=True)
    shifted = inputs - center
    spread = jnp.mean(shifted * shifted, axis=-1, keepdims=True)
    return shifted * lax.rsqrt(spread + NORM_EPS) * scale_gain


def rotary_tables(positions):
    half_size = HD // 2
    frequency = jnp.arange(half_size).astype(jnp.float32)
    inverse = ROPE_BASE ** (-2.0 * frequency / HD)
    first_end = HD // 8
    second = first_end + 3 * HD // 16
    ordinal = jnp.arange(half_size)
    section = jnp.where(ordinal < first_end, 0, jnp.where(ordinal < second, 1, 2))
    chosen = jnp.where(
        section[:, None] == 0,
        positions[0][None, :],
        jnp.where(section[:, None] == 1, positions[1][None, :], positions[2][None, :]),
    )
    angles = chosen.T.astype(jnp.float32) * inverse[None, :]
    return jnp.cos(angles), jnp.sin(angles)


def rotate(values, cosine, sine):
    rows = values.shape[0]
    heads = values.reshape(rows, -1, HD)
    upper = heads[..., : HD // 2]
    lower = heads[..., HD // 2 :]
    cosine = cosine[:, None, :]
    sine = sine[:, None, :]
    turned = jnp.concatenate([upper * cosine - lower * sine, lower * cosine + upper * sine], axis=-1)
    return turned.reshape(rows, -1)


def line_gather(block, size):
    place = lax.axis_index(TP)
    if size != 4:
        whole = lax.all_gather(block, TP, axis=0)
        return [whole[j] for j in range(size)]
    pair = lax.ppermute(block, TP, [(0, 1), (1, 0), (2, 3), (3, 2)])
    cross = lax.ppermute(block, TP, [(1, 2), (2, 1)])
    outer = lax.ppermute(cross, TP, [(1, 0), (2, 3)])
    cross_far = lax.ppermute(pair, TP, [(1, 2), (2, 1)])
    outer_far = lax.ppermute(cross_far, TP, [(1, 0), (2, 3)])
    at_end = (place == 0) | (place == 3)
    return [block, pair, jnp.where(at_end, outer, cross), jnp.where(at_end, outer_far, cross_far)]


def line_order(size):
    place = lax.axis_index(TP)
    if size != 4:
        same = jnp.arange(size, dtype=jnp.int32)
        return same, same
    return (
        jnp.asarray(LINE_BLOCKS)[place],
        jnp.asarray(np.argsort(LINE_BLOCKS, axis=1).astype(np.int32))[place],
    )


def handoff_tables(patch_counts, placement, width_wide, myself, capacity, rows, base=0):
    merged_count = patch_counts // 4
    owners = placement[:, 0]
    starts = placement[:, 1]
    owner_grid = owners.reshape(width_wide, IMG_DEV)
    count_grid = merged_count.reshape(width_wide, IMG_DEV)
    ordinal = jnp.arange(IMG_DEV)
    before = ordinal[:, None] < ordinal[None, :]
    same_owner = owner_grid[:, :, None] == owner_grid[:, None, :]
    offsets = jnp.sum(jnp.where(same_owner & before[None], count_grid[:, :, None], 0), axis=1)
    mine_owner = lax.dynamic_index_in_dim(owner_grid, myself, 0, keepdims=False)
    mine_count = lax.dynamic_index_in_dim(count_grid, myself, 0, keepdims=False)
    mine_offset = lax.dynamic_index_in_dim(offsets, myself, 0, keepdims=False)
    target = (jnp.arange(width_wide) ^ base)[:, None, None]
    slot_index = jnp.arange(capacity)[None, :, None]
    matches = (
        (mine_owner[None, None, :] == target)
        & (slot_index >= mine_offset[None, None, :])
        & (slot_index < mine_offset[None, None, :] + mine_count[None, None, :])
    )
    source_row = ordinal[None, None, :] * MAXM + slot_index - mine_offset[None, None, :]
    send_index = jnp.sum(jnp.where(matches, source_row, 0), axis=-1)
    row_place = jnp.arange(rows)[:, None]
    inside = (
        (owners[None, :] == myself)
        & (row_place >= starts[None, :])
        & (row_place < starts[None, :] + merged_count[None, :])
    )
    image_source = jnp.arange(owners.shape[0]) // IMG_DEV
    flat_slot = (
        (image_source ^ base)[None, :] * capacity
        + offsets.reshape(-1)[None, :]
        + row_place
        - starts[None, :]
    )
    take_index = jnp.sum(jnp.where(inside, flat_slot, 0), axis=-1)
    take_live = jnp.any(inside, axis=-1)
    return (send_index, take_index, take_live)


def gather_weights(shard, groups, width_wide):
    depth = shard.shape[0]
    mine = lax.axis_index(WIDE)
    if groups != 2 or width_wide != 4:
        whole = lax.all_gather(shard, WIDE, axis=0)
        return [(j, 0, whole[j]) for j in range(width_wide)]
    half = depth // 2
    group = lax.axis_index(GROUPS)
    core = [(0, 1), (1, 0), (2, 3), (3, 2)]
    part = lax.dynamic_slice_in_dim(shard, group * half, half, 0)
    first = lax.ppermute(part, WIDE, [(0, 2), (2, 0), (1, 3), (3, 1)])
    second = lax.ppermute(first, GROUPS, [(0, 1), (1, 0)])
    beside = lax.ppermute(shard, WIDE, core)
    first_beside = lax.ppermute(first, WIDE, core)
    second_beside = lax.ppermute(second, WIDE, core)
    return [
        (mine, 0, shard),
        (mine ^ 1, 0, beside),
        (mine ^ 2, group * half, first),
        (mine ^ 2, half - group * half, second),
        (mine ^ 3, group * half, first_beside),
        (mine ^ 3, half - group * half, second_beside),
    ]


def project(slots, places, gain, pieces):
    rows, width = slots[0].shape
    stacked = jnp.stack(slots)
    squares = sum(jnp.sum(jnp.square(s.astype(jnp.float32)), axis=-1) for s in slots)
    features = width * len(slots)
    scale = lax.rsqrt(squares / features + NORM_EPS)
    gain_blocks = gain.reshape(len(slots), width)
    total = None
    if len(pieces) == len(slots) or pieces[0][2].shape[0] == width:
        for block, first, weight in pieces:
            depth = weight.shape[0]
            part = lax.dynamic_slice(stacked, (places[block], 0, first), (1, rows, depth))[0]
            scaled = lax.dynamic_slice(gain_blocks, (block, first), (1, depth))
            part = (part.astype(jnp.float32) * scaled).astype(jnp.bfloat16)
            term = jnp.dot(part, weight, preferred_element_type=jnp.float32)
            total = term if total is None else total + term
    else:
        flat = jnp.concatenate([slots[j] for j in range(len(slots))], axis=1)
        flat = (flat.astype(jnp.float32) * gain).astype(jnp.bfloat16)
        weight = jnp.concatenate([p[2] for p in pieces], axis=0)
        total = jnp.dot(flat, weight, preferred_element_type=jnp.float32)
    return total * scale[:, None]


def per_device_any(
    patches,
    patch_counts,
    placement,
    positions,
    text_embeds,
    vit_gain,
    vit_qkv,
    vit_proj,
    merger_gain,
    merger_up,
    merger_down,
    llm_gain,
    llm_query,
    llm_key,
    llm_value,
):
    groups = lax.axis_size(GROUPS)
    width_wide = lax.axis_size(WIDE)
    size = lax.axis_size(TP)
    myself = lax.axis_index(WIDE)
    place = lax.axis_index(TP)
    _, places = line_order(size)
    width = patches.shape[1]
    capacity = MAXM * ((IMG_DEV + width_wide - 1) // width_wide)
    tokens = text_embeds.shape[0]
    local_heads = vit_qkv.shape[2] // VHD
    send_index, take_index, take_live = handoff_tables(
        patch_counts, placement, width_wide, myself, capacity, tokens
    )

    weight_shard = jnp.concatenate([llm_query, llm_key, llm_value], axis=1)
    pieces = gather_weights(weight_shard, groups, width_wide)
    text_slots = line_gather(text_embeds, size)

    patch_rows = patches.astype(jnp.float32)
    normed = layer_norm(patch_rows, vit_gain).astype(jnp.bfloat16)
    triple = jnp.dot(normed, vit_qkv.reshape(width, -1), preferred_element_type=jnp.float32)
    triple = triple.astype(jnp.bfloat16).reshape(IMG_DEV, MAXP, 3, local_heads, VHD)
    scores = jnp.einsum(
        "iqhd,ikhd->ihqk", triple[:, :, 0], triple[:, :, 1], preferred_element_type=jnp.float32
    ) * VHD ** (-0.5)
    own_counts = lax.dynamic_slice_in_dim(patch_counts, myself * IMG_DEV, IMG_DEV)
    present = jnp.arange(MAXP)[None, :] < own_counts[:, None]
    scores = jnp.where(present[:, None, None, :], scores, -jnp.inf)
    highest = jnp.max(scores, axis=-1, keepdims=True)
    raised = jnp.exp(scores - highest)
    probs = (raised / jnp.sum(raised, axis=-1, keepdims=True)).astype(jnp.bfloat16)
    context = jnp.einsum(
        "ihqk,ikhd->iqhd", probs, triple[:, :, 2], preferred_element_type=jnp.float32
    ).astype(jnp.bfloat16)
    context = context.reshape(IMG_DEV * MAXP, local_heads * VHD)
    partial_heads = jnp.dot(context, vit_proj, preferred_element_type=jnp.float32)

    share_rows = IMG_DEV * MAXP // size
    shares = partial_heads.astype(jnp.bfloat16).reshape(size, share_rows, width)
    shares = lax.all_to_all(shares, TP, split_axis=0, concat_axis=0, tiled=True)
    attended = jnp.sum(shares.astype(jnp.float32), axis=0)
    own_rows = lax.dynamic_slice_in_dim(patch_rows, place * share_rows, share_rows, 0)
    merged_rows = IMG_DEV * MAXM // size
    merged_in = layer_norm(own_rows + attended, merger_gain).astype(jnp.bfloat16)
    merged_in = merged_in.reshape(merged_rows, 4 * width)
    merged_all = jnp.concatenate(line_gather(merged_in, size), axis=0)
    hidden = jax.nn.gelu(
        jnp.dot(merged_all, merger_up, preferred_element_type=jnp.float32), approximate=False
    ).astype(jnp.bfloat16)
    picked = send_index.reshape(-1)
    picked = places[picked // merged_rows] * merged_rows + picked % merged_rows
    packed = jnp.take(hidden, picked, axis=0)
    partial_visual = jnp.dot(packed, merger_down, preferred_element_type=jnp.float32)
    slices = partial_visual.astype(jnp.bfloat16).reshape(width_wide, capacity, size, -1)
    slices = jnp.transpose(slices, (0, 2, 1, 3)).reshape(width_wide * size, capacity, -1)
    slices = lax.all_to_all(slices, (WIDE, TP), split_axis=0, concat_axis=0, tiled=True)
    visual = jnp.sum(slices.reshape(width_wide, size, capacity, -1).astype(jnp.float32), axis=1)
    visual = visual.astype(jnp.bfloat16).reshape(width_wide * capacity, -1)
    visual_slots = line_gather(visual, size)

    text_out = project(text_slots, places, llm_gain, pieces)
    visual_out = project(visual_slots, places, llm_gain, pieces)
    joined = jnp.where(take_live[:, None], jnp.take(visual_out, take_index, axis=0), text_out)
    cosine, sine = rotary_tables(positions)
    q_end = llm_query.shape[1]
    k_end = q_end + llm_key.shape[1]
    queries = rotate(joined[:, :q_end], cosine, sine).astype(jnp.bfloat16)
    key_rows = rotate(joined[:, q_end:k_end], cosine, sine).astype(jnp.bfloat16)
    value_rows = joined[:, k_end:].astype(jnp.bfloat16)
    return (queries, key_rows, value_rows)


ENDS = [(0, 1), (1, 0), (2, 3), (3, 2)]
MIDDLE = [(1, 2), (2, 1)]
OUTWARD = [(1, 0), (2, 3)]
ACROSS = [(0, 2), (2, 0), (1, 3), (3, 1)]
MINP = 24
TILE = 256
LINES = 16
PIECES = 2


def fetch_weights(state, slot, weights, buffer, sems, tiles):
    own, beside = weights[0:3], weights[3:6]
    far = weights[6 : 6 + 2 * PIECES]
    far_beside = weights[6 + 2 * PIECES :]
    where, group = state[slot], state[8]
    piece = far[0].shape[0]
    q_tiles = own[0].shape[1] // TILE
    for tile in range(tiles):
        columns = pl.ds(tile * TILE, TILE)
        for which, parts in ((0, own), (1, beside)):
            source = parts[0].at[:, columns] if tile < q_tiles else parts[1 + tile - q_tiles]

            @pl.when(where == which)
            def _():
                pltpu.make_async_copy(source, buffer.at[:, columns], sems.at[tile]).start()

        for which, parts in ((2, far), (3, far_beside)):

            @pl.when(where == which)
            def _():
                for rank in range(2):
                    for index in range(PIECES):
                        start = jnp.where(group == rank, 0, PIECES * piece) + index * piece
                        start = pl.multiple_of(start, piece)
                        pltpu.make_async_copy(
                            parts[rank * PIECES + index].at[:, columns],
                            buffer.at[pl.ds(start, piece), columns],
                            sems.at[tile],
                        ).start()


def compact_body(myself, counts, placement, text, gain, out_a, out_b, squares, partial):
    tokens, depth = text.shape
    images = counts.shape[1]
    kept = out_a.shape[0] + out_b.shape[0]
    eye = lax.broadcasted_iota(jnp.int32, (images, images), 0) == lax.broadcasted_iota(
        jnp.int32, (images, images), 1
    )
    as_col = lambda row: jnp.sum(jnp.where(eye, row, 0.0), axis=1, keepdims=True)
    merged = (counts[...] // 4).astype(jnp.float32)
    spots = placement[...].astype(jnp.float32)
    mine_row = (spots[0:1, :] == myself[0].astype(jnp.float32)).astype(jnp.float32)
    start_row = spots[1:2, :]
    count_row = merged * mine_row
    count_col = as_col(count_row)
    start_col = as_col(start_row)
    earlier = jnp.sum(jnp.where(start_col < start_row, count_col, 0.0), axis=0, keepdims=True)
    threshold = start_row - earlier
    order = lax.broadcasted_iota(jnp.int32, (kept, images), 0).astype(jnp.float32)
    rows = jnp.sum(jnp.where(order >= threshold, count_row, 0.0), axis=1, keepdims=True)
    rows = jnp.minimum(rows + order[:, 0:1], tokens - 1.0)
    lanes = lax.broadcasted_iota(jnp.int32, (kept, tokens), 1).astype(jnp.float32)
    select = (lanes == rows).astype(jnp.float32).astype(jnp.bfloat16)
    low = 0
    for out in (out_a, out_b):
        high = low + out.shape[0]
        for start in range(0, depth, TILE):
            columns = slice(start, start + TILE)
            chosen = jnp.dot(select[low:high], text[:, columns], preferred_element_type=jnp.float32)
            square = chosen * chosen
            square = sum(square[:, lane : lane + 128] for lane in range(0, TILE, 128))
            if start:
                square = square + partial[low:high, :]
            partial[low:high, :] = square
            out[:, columns] = (chosen * gain[:, columns]).astype(jnp.bfloat16)
        low = high
    totals = lax.dot_general(
        jnp.ones((8, 128), jnp.float32),
        partial[...],
        (((1,), (1,)), ((), ())),
        precision=lax.Precision.HIGHEST,
        preferred_element_type=jnp.float32,
    )
    lines = []
    for start in range(0, kept, 128):
        line = totals[0:1, start : start + 128]
        if line.shape[1] < 128:
            line = jnp.concatenate([line, jnp.zeros((1, 128 - line.shape[1]), jnp.float32)], axis=1)
        lines.append(line)
    lines += [jnp.zeros((1, 128), jnp.float32)] * (squares.shape[0] // 4 - len(lines))
    coarse = [line.astype(jnp.bfloat16).astype(jnp.float32) for line in lines]
    lines = coarse + [line - near for line, near in zip(lines, coarse)]
    lines.append(jnp.zeros((squares.shape[0] - len(lines), 128), jnp.float32))
    squares[...] = jnp.zeros(squares.shape, squares.dtype)
    squares[:, :128] = jnp.concatenate(lines, axis=0).astype(jnp.bfloat16)


def compact_call(myself, counts, placement, text, gain, rows, width):
    whole = lambda x: pl.BlockSpec(x.shape, lambda i: (0,) * len(x.shape))
    tokens, depth = text.shape
    out = (
        jax.ShapeDtypeStruct((rows[0], depth), jnp.bfloat16),
        jax.ShapeDtypeStruct((rows[1], depth), jnp.bfloat16),
        jax.ShapeDtypeStruct((LINES, width), jnp.bfloat16),
    )
    inputs = (counts, placement, text, gain)
    return pl.pallas_call(
        compact_body,
        grid=(1,),
        out_shape=out,
        in_specs=[pl.BlockSpec(memory_space=pltpu.SMEM)] + [whole(x) for x in inputs],
        out_specs=tuple(whole(x) for x in out),
        scratch_shapes=[pltpu.VMEM((sum(rows), 128), jnp.float32)],
        cost_estimate=pl.CostEstimate(
            flops=2 * tokens * sum(rows) * depth, bytes_accessed=4 * tokens * depth, transcendentals=0
        ),
    )(myself, *inputs)


def row_scale(lines, low, rows, features):
    eye = lax.broadcasted_iota(jnp.int32, (128, 128), 0) == lax.broadcasted_iota(
        jnp.int32, (128, 128), 1
    )
    columns = []
    for start in range(low, low + rows, 128):
        line = lines[start // 128 : start // 128 + 1, :]
        columns.append(jnp.sum(jnp.where(eye, line, 0.0), axis=1, keepdims=True))
    column = jnp.concatenate(columns, axis=0)[:rows]
    return lax.rsqrt(column / features + NORM_EPS)


def rope_rows(total, factor, cosine, sine, q_columns, k_columns, result):
    cos, sin = cosine[...], sine[...]
    columns = total.shape[1]
    for low in range(0, columns, HD):
        values = total[:, low : low + HD] * factor
        if low < q_columns + k_columns:
            values = values * cos + pltpu.roll(values, HD // 2, 1) * sin
        result[:, low : low + HD] = values.astype(jnp.bfloat16)


def load_rows(state, candidates, rows, scaled, sem):
    for index, parts in enumerate(candidates):
        low = 0
        for part, count in zip(parts, rows):
            copy = pltpu.make_async_copy(part, scaled.at[pl.ds(low, count), :], sem)
            if len(candidates) == 1:
                copy.start()
            else:
                pl.when(state[9] == 1 - index)(copy.start)
            low += count


def matmul_slot(scaled, buffer, sems, total, before, tiles):
    def multiply(tile, carry):
        columns = pl.ds(pl.multiple_of(tile * TILE, TILE), TILE)
        if sems is not None:
            target = buffer.at[:, columns]
            pltpu.make_async_copy(target, target, sems.at[tile]).wait()
        term = jnp.dot(scaled[...], buffer[:, columns], preferred_element_type=jnp.float32)
        if before is not None:
            term = term + before[:, columns]
        total[:, columns] = term
        return carry

    lax.fori_loop(0, tiles, multiply, 0)


def text_body(plan, *refs):
    refs = list(refs)
    take = lambda count: [refs.pop(0) for _ in range(count)]
    (state,) = take(1)
    rows = plan.rows
    texts = [[take(len(rows)) for _ in range(count)] for count in plan.candidates]
    finish = plan.finish
    weights = take(1 if finish == 2 else 6 + 4 * PIECES)
    before = take(1)[0].at[pl.ds(plan.low, sum(rows)), :] if plan.has_sum else None
    if finish:
        lines, cosine, sine = take(3)
    if finish == 1:
        ready, block = take(2)
    elif finish == 2:
        groups = take(2)
        places = take(3)
        results = take(3)
    else:
        (total,) = take(1)
    scaled, load_sems = take(2)
    if finish == 2:
        total, turned = take(2)
        buffer, sems = weights[0], None
    elif finish == 1:
        sems, total = take(2)
        buffer = block
    else:
        buffer, sems = take(2)
    tiles = plan.tiles
    slots = len(texts)
    if finish == 1:
        fetch_weights(state, 0, weights, buffer, sems.at[0], tiles)
    elif not finish:
        fetch_weights(state, 0, weights, buffer.at[0], sems.at[0], tiles)
    load_rows(state, texts[0], rows, scaled.at[0], load_sems.at[0])
    for slot in range(slots):
        now, after = slot % 2, (slot + 1) % 2
        if slot + 1 < slots:
            fetch_weights(state, slot + 1, weights, buffer.at[after], sems.at[after], tiles)
            load_rows(state, texts[slot + 1], rows, scaled.at[after], load_sems.at[after])
        pltpu.make_async_copy(scaled.at[now], scaled.at[now], load_sems.at[now]).wait()
        matmul_slot(
            scaled.at[now],
            buffer if finish else buffer.at[now],
            None if sems is None else sems.at[now],
            total,
            total if slot else before,
            tiles,
        )

    q_columns, k_columns = plan.heads
    if not finish:
        pass
    elif finish == 1:
        scale = row_scale(lines, plan.low, sum(rows), plan.features)
        rope_rows(total, scale, cosine, sine, q_columns, k_columns, ready)
    else:
        scale = row_scale(lines, plan.low, sum(rows), plan.features)
        rope_rows(total, scale, cosine, sine, q_columns, k_columns, turned)
        parts = (groups[0], turned, groups[1])
        for low in range(0, total.shape[1], TILE):
            placed = None
            for place, group in zip(places, parts):
                term = jnp.dot(
                    place[...], group[:, low : low + TILE], preferred_element_type=jnp.float32
                )
                placed = term if placed is None else placed + term
            placed = placed.astype(jnp.bfloat16)
            if low < q_columns:
                results[0][:, low : low + TILE] = placed
            elif low < q_columns + k_columns:
                results[1][:, low - q_columns : low - q_columns + TILE] = placed
            else:
                start = low - q_columns - k_columns
                results[2][:, start : start + TILE] = placed


def visual_body(plan, *refs):
    refs = list(refs)
    take = lambda count: [refs.pop(0) for _ in range(count)]
    state, own, one, two, three, gain = take(6)
    weights = take(6 + 4 * PIECES)
    cosine, sine, ready, scaled, buffer, sems, total = take(7)
    tiles = plan.tiles
    blocks, rows, depth = scaled.shape
    fetch_weights(state, 0, weights, buffer.at[0], sems.at[0], tiles)
    squares = jnp.zeros((rows, 1), jnp.float32)
    for block in range(blocks):
        ends, middle = (one, own) if block < blocks // 2 else (three, two)
        low = block % (blocks // 2) * depth
        columns = slice(low, low + depth)
        text = jnp.where(
            state[9] == 1,
            ends[:, columns].astype(jnp.float32),
            middle[:, columns].astype(jnp.float32),
        )
        squares = squares + jnp.sum(text * text, axis=-1, keepdims=True)
        scaled[block] = (text * gain[pl.ds(state[4 + block], 1), :]).astype(jnp.bfloat16)
    for slot in range(blocks):
        if slot + 1 < blocks:
            after = (slot + 1) % 2
            fetch_weights(state, slot + 1, weights, buffer.at[after], sems.at[after], tiles)
        now = slot % 2
        matmul_slot(
            scaled.at[slot], buffer.at[now], sems.at[now], total, total if slot else None, tiles
        )
    scale = lax.rsqrt(squares / (blocks * depth) + NORM_EPS)
    rope_rows(total, scale, cosine, sine, *plan.heads, ready)


def product_call(
    state, texts, weights, rows, visual=None, before=None, finish=0, extra=(), out=(), limit=40, low=0, features=0
):
    if finish == 2:
        heads = (out[0].shape[1], out[1].shape[1])
    else:
        heads = (weights[0].shape[1], weights[1].shape[1])
    columns = weights[0].shape[1] if finish == 2 else 2 * heads[1] + heads[0]
    depth = weights[0].shape[0]
    tiles = columns // TILE
    every = sum(rows)
    whole = lambda x: pl.BlockSpec(x.shape, lambda i: (0,) * len(x.shape))
    anywhere = pl.BlockSpec(memory_space=pltpu.HBM)
    plan = SimpleNamespace(rows=rows, has_sum=before is not None, finish=finish, tiles=tiles, heads=heads)
    plan.low, plan.features = low, features
    late = [*(() if before is None else (before,)), *extra]
    if visual is None:
        slots = len(texts)
        plan.candidates = [len(t) for t in texts]
        flat = [part for slot in texts for candidate in slot for part in candidate]
        specs = [anywhere] * len(flat)
        function = text_body
        loads = [pltpu.VMEM((2, every, depth), jnp.bfloat16), pltpu.SemaphoreType.DMA((2,))]
    else:
        slots = visual[-1].shape[0]
        flat = list(visual)
        specs = [whole(x) for x in flat]
        function = visual_body
        loads = [pltpu.VMEM((slots, every, depth), jnp.bfloat16)]
    inside = pl.BlockSpec(memory_space=pltpu.VMEM)
    specs = [pl.BlockSpec(memory_space=pltpu.SMEM)] + specs
    specs += [inside if finish == 2 else anywhere] * len(weights)
    specs += [inside if finish else whole(x) for x in late]
    depth_of = min(2, slots)
    sums = pltpu.VMEM((every, columns), jnp.float32)
    sems = pltpu.SemaphoreType.DMA((depth_of, tiles))
    if finish == 2:
        scratch = loads + [sums, pltpu.VMEM((every, columns), jnp.bfloat16)]
    elif finish == 1:
        scratch = loads + [sems, sums]
    else:
        scratch = loads + [pltpu.VMEM((depth_of, depth, columns), jnp.bfloat16), sems]
        if visual is not None:
            scratch.append(sums)
    if not out:
        out = (pltpu.VMEM((every, columns), jnp.float32),)

    def body(*refs):
        function(plan, *refs)

    return pl.pallas_call(
        body,
        grid=(1,),
        out_shape=out,
        in_specs=specs,
        out_specs=tuple(whole(x) if finish == 2 else inside for x in out),
        scratch_shapes=scratch,
        compiler_params=pltpu.CompilerParams(vmem_limit_bytes=limit << 20),
        cost_estimate=pl.CostEstimate(
            flops=2 * every * depth * columns * slots,
            bytes_accessed=2 * depth * columns * slots,
            transcendentals=0,
        ),
    )(state, *flat, *weights, *late)


def run_kernel(body, operands, specs, out, flops, scratch=(), limit=24):
    whole = lambda x: pl.BlockSpec(x.shape, lambda i: (0,) * len(x.shape))
    specs = [whole(x) if spec is None else spec for x, spec in zip(operands, specs)]
    return pl.pallas_call(
        body,
        grid=(1,),
        out_shape=out,
        in_specs=specs,
        out_specs=tuple(whole(x) for x in out),
        scratch_shapes=scratch,
        compiler_params=pltpu.CompilerParams(vmem_limit_bytes=limit << 20),
        cost_estimate=pl.CostEstimate(
            flops=flops, bytes_accessed=2 * sum(x.size for x in operands), transcendentals=0
        ),
    )(*operands)


def heads_body(state, context, weight, squares, near, far):
    half = context.shape[0] // 2
    for out, flank in ((near, state[0]), (far, 1 - state[0])):
        rows = context[pl.ds(pl.multiple_of(flank * half, half), half), :]
        share = jnp.dot(rows, weight[...], preferred_element_type=jnp.float32)
        out[:half, :] = share.astype(jnp.bfloat16)
        out[half:, :] = squares[...]


def mixer_body(state, near, one, two, three, patches, gain, out, normed):
    half = patches.shape[0] // 2
    width = patches.shape[1]
    total = sum(part[:half, :].astype(jnp.float32) for part in (near, one, two, three))
    own = patches[pl.ds(pl.multiple_of(state[0] * half, half), half), :].astype(jnp.float32)
    mixed = own + total
    shifted = mixed - jnp.mean(mixed, axis=-1, keepdims=True)
    spread = jnp.mean(shifted * shifted, axis=-1, keepdims=True)
    scaled = shifted * lax.rsqrt(spread + NORM_EPS) * gain[...]
    rows = out.shape[0]
    for lane in range(0, width, 128):
        normed[lane // 128] = scaled[:, lane : lane + 128]
    for index in range(4):
        for lane in range(0, width, 128):
            joined = normed[lane // 128, pl.ds(index, rows, stride=4), :]
            low = index * width + lane
            out[:, low : low + 128] = joined.astype(jnp.bfloat16)
    tails = sum(part[half:, :128].astype(jnp.float32) for part in (near, one, two, three))
    count = LINES // 4
    lines = tails[:count] + tails[count : 2 * count]
    coarse = lines.astype(jnp.bfloat16).astype(jnp.float32)
    rest = jnp.zeros((rows - 2 * count, 128), jnp.float32)
    tails = jnp.concatenate([coarse, lines - coarse, rest], axis=0)
    out[:, 4 * width :] = tails.astype(jnp.bfloat16)


def merger_body(state, own, one, two, three, pack, up, *outs):
    packs, lines = outs[:-1], outs[-1]
    at_end = state[1] == 1
    inner = up.shape[0]
    pick = lambda a, b: jnp.where(at_end, a[...].astype(jnp.float32), b[...].astype(jnp.float32))
    near, far = pick(one, own), pick(three, two)
    count = LINES // 4
    lines[...] = jnp.zeros(lines.shape, jnp.float32)
    lines[0:count, :] = near[0:count, inner:] + near[count : 2 * count, inner:]
    rows = jnp.concatenate([near[:, :inner], far[:, :inner]], axis=0).astype(jnp.bfloat16)
    before = jnp.dot(rows, up[...], preferred_element_type=jnp.float32)
    hidden = 0.5 * before * (1.0 + lax.erf(before * (0.5**0.5)))
    packed = jnp.dot(
        pack[...], hidden.astype(jnp.bfloat16), preferred_element_type=jnp.float32
    ).astype(jnp.bfloat16)
    capacity = packs[0].shape[0]
    for index, out in enumerate(packs):
        out[...] = packed[index * capacity : (index + 1) * capacity]


def down_body(state, zero, one, two, three, down, near, far):
    hidden = jnp.concatenate([part[...] for part in (zero, one, two, three)], axis=0)
    half = near.shape[1]
    step = 2 * TILE

    def multiply(index, carry):
        here = pl.ds(pl.multiple_of(index * step, step), step)
        for out, flank in ((near, state[0]), (far, 1 - state[0])):
            there = pl.ds(pl.multiple_of(flank * half + index * step, step), step)
            share = jnp.dot(hidden, down[:, there], preferred_element_type=jnp.float32)
            out[:, here] = share.astype(jnp.bfloat16)
        return carry

    lax.fori_loop(0, half // step, multiply, 0)


def sum_body(zero, one, two, three, out):
    total = sum(part[...].astype(jnp.float32) for part in (zero, one, two, three))
    out[...] = total.astype(jnp.bfloat16)


def to_middle(near, far):
    return [
        lax.ppermute(near, TP, [(0, 1), (3, 2)]),
        lax.ppermute(far, TP, MIDDLE),
        lax.ppermute(far, TP, [(0, 2), (3, 1)]),
    ]


def from_middle(half, hop):
    crossed = lax.ppermute(half, TP, MIDDLE)
    return [
        lax.ppermute(half, TP, OUTWARD),
        crossed,
        lax.ppermute(crossed, TP, OUTWARD)
        if hop
        else lax.ppermute(half, TP, [(1, 3), (2, 0)]),
    ]


def resident_call(*arrays):
    def body(*refs):
        count = len(arrays)
        sems = refs[2 * count]
        copies = [
            pltpu.make_async_copy(refs[i], refs[count + i], sems.at[i]) for i in range(count)
        ]
        for copy in copies:
            copy.start()
        for copy in copies:
            copy.wait()

    return pl.pallas_call(
        body,
        out_shape=tuple(pltpu.VMEM(x.shape, x.dtype) for x in arrays),
        in_specs=[pl.BlockSpec(memory_space=pl.ANY)] * len(arrays),
        out_specs=tuple(pl.BlockSpec(memory_space=pltpu.VMEM) for _ in arrays),
        scratch_shapes=[pltpu.SemaphoreType.DMA((len(arrays),))],
        compiler_params=pltpu.CompilerParams(vmem_limit_bytes=32 << 20),
        cost_estimate=pl.CostEstimate(
            flops=0, bytes_accessed=sum(2 * x.size for x in arrays), transcendentals=0
        ),
    )(*arrays)


def text_columns(patch_counts, placement, myself, tokens):
    counts = jnp.where(placement[:, 0] == myself, patch_counts // 4, 0)
    starts = placement[:, 1]
    place = jnp.arange(tokens)
    return place - jnp.sum(jnp.where(place[:, None] >= starts[None, :], counts[None, :], 0), axis=1)


def per_device(
    patches,
    patch_counts,
    placement,
    positions,
    text_embeds,
    vit_gain,
    vit_qkv,
    vit_proj,
    merger_gain,
    merger_up,
    merger_down,
    llm_gain,
    llm_query,
    llm_key,
    llm_value,
):
    width_wide = lax.axis_size(WIDE)
    size = lax.axis_size(TP)
    myself = lax.axis_index(WIDE)
    place = lax.axis_index(TP)
    side = lax.axis_index(GROUPS)
    width = patches.shape[1]
    capacity = MAXM * ((IMG_DEV + width_wide - 1) // width_wide)
    tokens, depth = text_embeds.shape
    local_heads = vit_qkv.shape[2] // VHD
    send_index, take_index, take_live = handoff_tables(
        patch_counts, placement, width_wide, myself, capacity, tokens, myself
    )
    flank = (place >= size // 2).astype(jnp.int32)
    at_end = ((place == 0) | (place == size - 1)).astype(jnp.int32)
    spot = jnp.stack([flank, at_end])
    scalars = pl.BlockSpec(memory_space=pltpu.SMEM)
    inside = pl.BlockSpec(memory_space=pltpu.VMEM)
    bf16 = lambda *shape: jax.ShapeDtypeStruct(shape, jnp.bfloat16)

    blocks = jnp.asarray(LINE_BLOCKS)[place]
    gain_blocks = llm_gain.reshape(size, depth)
    kept = tokens - IMG_DEV * (MINP // 4)
    rows_a = (kept // 2 + 127) // 128 * 128
    rows = [rows_a, kept - rows_a]
    text_a, text_b, squares = compact_call(
        myself.reshape(1),
        patch_counts.reshape(1, -1),
        placement.T,
        text_embeds,
        lax.dynamic_slice_in_dim(gain_blocks, place, 1, 0),
        rows,
        width,
    )
    near_a = lax.ppermute(text_a, TP, ENDS)
    middle_a = lax.ppermute(text_a, TP, MIDDLE)

    slots = width_wide * capacity
    back = text_columns(patch_counts, placement, myself, tokens)
    column = jnp.where(take_live, kept + take_index, back)
    select = column[:, None] == jnp.arange(kept + slots)[None, :]
    cuts = [(0, rows[0]), (rows[0], kept), (kept, kept + slots)]
    places = [
        (column[:, None] == jnp.arange(low, high)[None, :]).astype(jnp.bfloat16)
        for low, high in cuts
    ]
    spots = jnp.sum(jnp.where(select[None], positions[:, :, None], 0), axis=1)
    cosine, sine = rotary_tables(spots)
    cosine = jnp.concatenate([cosine, cosine], axis=1)
    sine = jnp.concatenate([-sine, sine], axis=1)
    cosines = [cosine[low:high] for low, high in cuts]
    sines = [sine[low:high] for low, high in cuts]
    picked = send_index.reshape(-1)
    half_rows = IMG_DEV * MAXM // 2
    picked = ((picked // half_rows) ^ flank) * half_rows + picked % half_rows
    pack = (picked[:, None] == jnp.arange(2 * half_rows)[None, :]).astype(jnp.bfloat16)
    tables = (cosines, sines, pack)

    patch_rows = patches.astype(jnp.float32)
    normed = layer_norm(patch_rows, vit_gain).astype(jnp.bfloat16)
    triple = jnp.dot(normed, vit_qkv.reshape(width, -1), preferred_element_type=jnp.float32)
    triple = triple.astype(jnp.bfloat16).reshape(IMG_DEV, MAXP, 3, local_heads, VHD)
    scores = jnp.einsum(
        "iqhd,ikhd->ihqk", triple[:, :, 0], triple[:, :, 1], preferred_element_type=jnp.float32
    ) * VHD ** (-0.5)
    own_counts = lax.dynamic_slice_in_dim(patch_counts, myself * IMG_DEV, IMG_DEV)
    present = jnp.arange(MAXP)[None, :] < own_counts[:, None]
    scores = jnp.where(present[:, None, None, :], scores, -jnp.inf)
    highest = jnp.max(scores, axis=-1, keepdims=True)
    raised = jnp.exp(scores - highest)
    probs = (raised / jnp.sum(raised, axis=-1, keepdims=True)).astype(jnp.bfloat16)
    context = jnp.einsum(
        "ihqk,ikhd->iqhd", probs, triple[:, :, 2], preferred_element_type=jnp.float32
    ).astype(jnp.bfloat16)
    context = context.reshape(IMG_DEV * MAXP, local_heads * VHD)
    half_patches = IMG_DEV * MAXP // 2
    near, far = run_kernel(
        heads_body, [spot, context, vit_proj, squares], [scalars, None, None, None],
        (bf16(half_patches + LINES, width), bf16(half_patches + LINES, width)),
        2 * IMG_DEV * MAXP * vit_proj.size,
    )
    shares = to_middle(near, far)
    near_b = lax.ppermute(text_b, TP, ENDS)
    middle_b = lax.ppermute(text_b, TP, MIDDLE)
    piece = depth // (2 * PIECES)
    first, second, first_beside, second_beside = [], [], [], []
    for index in range(PIECES):
        part = jnp.concatenate(
            [
                lax.dynamic_slice_in_dim(w, (side * PIECES + index) * piece, piece, 0)
                for w in (llm_query, llm_key, llm_value)
            ],
            axis=1,
        )
        first.append(lax.ppermute(part, WIDE, ACROSS))
        second.append(lax.ppermute(first[index], GROUPS, [(0, 1), (1, 0)]))
        first_beside.append(lax.ppermute(first[index], WIDE, ENDS))
        second_beside.append(lax.ppermute(second[index], WIDE, ENDS))
    beside = [lax.ppermute(w, WIDE, ENDS) for w in (llm_query, llm_key, llm_value)]
    arrived = [*beside, *first, *second, *first_beside, *second_beside]
    arrived = [pltpu.with_memory_space_constraint(x, pltpu.HBM) for x in arrived]
    weights = [llm_query, llm_key, llm_value, *arrived]
    (merged_in,) = run_kernel(
        mixer_body, [spot, near, *shares, patches, merger_gain[None]],
        [scalars] + [None] * 6, (bf16(half_rows, 4 * width + 128),), 0,
        scratch=[pltpu.VMEM((width // 128, half_patches, 128), jnp.float32)],
    )
    merged_all = from_middle(merged_in, False)
    merged_all[0], tables, places = lax.optimization_barrier((merged_all[0], tables, places))
    cosines, sines, pack = tables
    outer_a = lax.ppermute(middle_a, TP, OUTWARD)
    far_a = lax.ppermute(near_a, TP, MIDDLE)
    up, down = resident_call(merger_up, merger_down)
    *packed, lines = run_kernel(
        merger_body, [spot, merged_in, *merged_all, pack, up],
        [scalars] + [None] * 5 + [inside],
        (bf16(capacity, up.shape[1]),) * width_wide + (jax.ShapeDtypeStruct((8, 128), jnp.float32),),
        4 * half_rows * up.size,
    )
    for step in range(1, width_wide):
        swap = [(i, i ^ step) for i in range(width_wide)]
        packed[step] = lax.ppermute(packed[step], WIDE, swap)
    near, far = run_kernel(
        down_body, [spot, *packed, down], [scalars] + [None] * width_wide + [inside],
        (bf16(slots, down.shape[1] // 2), bf16(slots, down.shape[1] // 2)),
        2 * slots * down.size,
    )
    shares = [near, *to_middle(near, far)]
    outer_b = lax.ppermute(middle_b, TP, OUTWARD)
    far_b = lax.ppermute(near_b, TP, MIDDLE)
    (visual,) = run_kernel(sum_body, shares, [None] * 4, (bf16(*near.shape),), 0, limit=16)
    visual_all = [visual, *from_middle(visual, True)]
    last_a = lax.ppermute(far_a, TP, OUTWARD)
    last_b = lax.ppermute(far_b, TP, OUTWARD)

    def state_of(chosen):
        chosen = jnp.concatenate([chosen, jnp.zeros((4 - chosen.shape[0],), jnp.int32)])
        rest = jnp.stack([side, at_end, jnp.int32(size * depth)])
        return jnp.concatenate([myself ^ chosen, chosen, rest]).astype(jnp.int32)

    every = jnp.arange(size, dtype=jnp.int32) ^ (flank * (size // 2))
    q_columns, k_columns, v_columns = (w.shape[1] for w in weights[:3])
    columns = q_columns + k_columns + v_columns
    early = [[[text_a, text_b]], [[near_a, near_b]], [[outer_a, outer_b], [middle_a, middle_b]]]
    held = lambda x: pltpu.with_memory_space_constraint(x, pltpu.HBM)
    early = [[[held(part) for part in parts] for parts in slot] for slot in early]
    (sums,) = product_call(state_of(blocks[:2]), early[:2], weights, rows, limit=26)
    (sums,) = product_call(state_of(blocks[2:3]), early[2:], weights, rows, before=sums, limit=20)
    (ready_seen,) = product_call(
        state_of(every), None, weights, [slots], visual=(*visual_all, gain_blocks),
        extra=(cosines[2], sines[2]), out=(pltpu.VMEM((slots, columns), jnp.bfloat16),), limit=26,
    )
    last = state_of(blocks[3:])
    ready_a, block = product_call(
        last, [[[held(last_a)], [held(far_a)]]], weights, rows[:1], before=sums, finish=1,
        extra=(lines, cosines[0], sines[0]), features=size * depth, limit=16,
        out=(pltpu.VMEM((rows[0], columns), jnp.bfloat16), pltpu.VMEM((depth, columns), jnp.bfloat16)),
    )
    return product_call(
        last, [[[held(last_b)], [held(far_b)]]], [block], rows[1:], before=sums, finish=2,
        extra=(lines, cosines[1], sines[1], ready_a, ready_seen, *places), low=rows[0],
        features=size * depth, limit=20,
        out=(bf16(tokens, q_columns), bf16(tokens, k_columns), bf16(tokens, v_columns)),
    )


def solution(mesh):
    shape = mesh.shape
    quick = shape[GROUPS] == 2 and shape[WIDE] == 4 and shape[TP] == 4
    return jax.shard_map(
        per_device if quick else per_device_any,
        mesh=mesh,
        in_specs=(
            P((GROUPS, WIDE), None),
            P(GROUPS),
            P(GROUPS, None),
            P(None, (GROUPS, WIDE)),
            P((GROUPS, WIDE), TP),
            P(),
            P(None, None, TP),
            P(TP, None),
            P(),
            P(None, TP),
            P(TP, None),
            P(),
            P(WIDE, TP),
            P(WIDE, TP),
            P(WIDE, TP),
        ),
        out_specs=(
            P((GROUPS, WIDE), TP),
            P((GROUPS, WIDE), TP),
            P((GROUPS, WIDE), TP),
        ),
        check_vma=False,
    )
```
